256 devices in a mesh: space: 32 (over y, z_lo, core), event: 8 (over x, z_hi).
Axes of the slice: x: 4, y: 4, z: 8 (z_hi: 2, z_lo: 4; z = z_hi * 4 + z_lo), core: 2. Of those that a mesh axis runs over, the one named last changes fastest.
Arguments:
- fwd_now: float32 [16, 64, 32768], P('event', None, 'space'), as said below
- fwd_prev: float32 [16, 64, 32768], P('event', None, 'space'), as said below
- adj_now: float32 [16, 64, 32768], P('event', None, 'space'), as said below
- adj_prev: float32 [16, 64, 32768], P('event', None, 'space'), as said below
- shear_mod: float32 [64, 32768], P(None, 'space'), may hold values from 0.5 to 2
- density: float32 [32768], P('space'), may hold values from 0.5 to 2
- station_owner: int32 [65536, 1], P('space'), may hold values from 0 to 31; in each aligned block of 2048 rows (0 to 2047, 2048 to 4095, ...) at most 256 rows name the same one
- receiver_local: int32 [65536], P('space'), may hold values from 0 to 1023
- station_weights: float32 [64, 65536], P(None, 'space'), may hold values from -6 to 6
- adj_records: float32 [16, 2, 65536], P('event', None, 'space'), may hold values from -6 to 6
Outputs:
- fwd_last: float32 [16, 64, 32768], P('event', None, 'space')
- fwd_before: float32 [16, 64, 32768], P('event', None, 'space')
- adj_last: float32 [16, 64, 32768], P('event', None, 'space')
- adj_before: float32 [16, 64, 32768], P('event', None, 'space')
- kernel: float32 [64, 32768], P(None, ('space', 'event'))
The draws below stay inside these ranges and needn't reach their ends.
Inputs may be any that keep to these rules, and one draw needn't show every extreme that they name: `station_owner`: the 2048 stations of one index of space name at most 256 with the same owner. `fwd_now`: each displacement is continuous: element-local copies of a shared node hold equal values. `fwd_prev`: continuous like fwd_now. `adj_now`: continuous like fwd_now. `adj_prev`: continuous like fwd_now.
All inputs are finite; a program needn't handle non-finite values.
Results may differ from the reference program's by a relative error of at most 0.0001.
Values sent between devices are 32-bit elements; how exact they have to be, the bound alone decides.
A program may use at most 64 MiB of HBM per device.

```python
import math
import jax
import jax.numpy as jnp
import numpy as np
from jax import lax

NODES = 64
EX = 16
EY = 16
LAYERS = 4
ST_DEV = 2048
STEPS = 2
CAP = 256
ELEM_DEV = 1024
ELEMENTS = 32768
EVENTS = 16
STATIONS = 65536
N_SPACE = 32


def nodal_field(key):
    depth = ELEMENTS // (EX * EY)
    shape = (EVENTS, 3 * depth + 1, 3 * EY + 1, 3 * EX + 1)
    values = jax.random.normal(key, shape, jnp.float32)
    element = jnp.arange(ELEMENTS, dtype=jnp.int32)
    node = jnp.arange(64, dtype=jnp.int32)
    col_x = 3 * (element % EX)[None, :] + (node % 4)[:, None]
    col_y = 3 * (element // EX % EY)[None, :] + (node // 4 % 4)[:, None]
    col_z = 3 * (element // (EX * EY))[None, :] + (node // 16)[:, None]
    return values[:, col_z, col_y, col_x]


def draw_fwd_now(key, part):
    return nodal_field(jax.random.fold_in(key, 11))


def draw_fwd_prev(key, part):
    return nodal_field(jax.random.fold_in(key, 23))


def draw_adj_now(key, part):
    return nodal_field(jax.random.fold_in(key, 37))


def draw_adj_prev(key, part):
    return nodal_field(jax.random.fold_in(key, 41))


def plant(result, key, least, top_value):
    longest = result.shape.index(max(result.shape))
    spots = []
    for shift in (0, 1):
        where = [jax.random.randint(jax.random.fold_in(key, axis), (), 0, length) for axis, length in enumerate(result.shape)]
        where[longest] = (where[longest] + shift) % result.shape[longest]
        spots.append(tuple(where))
    return result.at[spots[0]].set(least).at[spots[1]].set(top_value)


def block_scale(stream_key, extent, split, low, top_value):
    def one(axis_at, blocks):
        draws = jax.random.uniform(jax.random.fold_in(jax.random.fold_in(stream_key, 6), axis_at), (blocks,), jnp.float32, low / len(split), top_value / len(split))
        return jnp.repeat(jnp.exp(draws), extent[axis_at] // blocks).reshape((-1,) + (1,) * (len(extent) - axis_at - 1))

    factor_of = one(*split[0])
    for cut in split[1:]:
        factor_of = factor_of * one(*cut)
    return factor_of


def deal_out(stream_key, own, number, rows, amount, top, limit, lean):
    sequence = jax.random.permutation(stream_key, amount)
    heavy_load, ordinary = load_shares(amount, rows * top, limit, lean, True), load_shares(amount, rows * top, limit, lean, False)
    places = jnp.arange(amount)

    def named(lengths, rotation):
        used = int((lengths > 0).sum())
        fixed = max(1, used // 4)
        passed = fixed + (places - fixed + rotation * (used - fixed)) % max(1, amount - fixed)
        return jnp.zeros((amount,), jnp.int32).at[sequence[jnp.where(places < fixed, places, passed)]].set(jnp.asarray(lengths, jnp.int32))

    lengths = jnp.where(number % 4 == 0, named(heavy_load, number // 4), named(ordinary, number - number // 4 - 1))
    mixed = jax.random.permutation(jax.random.fold_in(own, 3), amount)
    source_of, receiver = mixed[0:amount // 2 * 2:2], mixed[1:amount // 2 * 2:2]
    slack = jnp.minimum(lengths[source_of] - 1, limit - lengths[receiver]) // 2
    slack = jnp.where((source_of == sequence[0]) | (receiver == sequence[0]) | (lengths[receiver] == 0), 0, jnp.maximum(slack, 0))
    passed = jax.random.randint(jax.random.fold_in(own, 4), (amount // 2,), 0, 1 << 20) % (slack + 1)
    lengths = lengths.at[source_of].add(-passed).at[receiver].add(passed)
    members = jnp.searchsorted(jnp.cumsum(lengths), jnp.arange(rows * top), side="right").astype(jnp.int32)
    listing = members.reshape(top, rows).T
    listing = listing[jax.random.permutation(jax.random.fold_in(own, 1), rows)]
    rotation = jax.random.randint(jax.random.fold_in(own, 2), (rows, 1), 0, top)
    return jnp.take_along_axis(listing, (jnp.arange(top)[None, :] + rotation) % top, axis=1)


def load_shares(amount, total, limit, slope, full):
    portions = [(1 << 20) // math.isqrt(standing ** slope) + 1 for standing in range(1, amount + 1)]
    largest = limit if full else min(limit, max(-(-total // amount), total * portions[0] // sum(portions)))
    least = 1 if total - largest >= amount - 1 else 0
    counts, rest = [largest] + [least] * (amount - 1), total - largest - least * (amount - 1)
    while rest > 0:
        movable = [i for i in range(1, amount) if counts[i] < largest] or [i for i in range(1, amount) if counts[i] < limit]
        pool, remaining = sum([portions[i] for i in movable]), rest
        for i in movable:
            more = min(limit - counts[i], max(1, remaining * portions[i] // pool), rest)
            counts[i] = counts[i] + more
            rest = rest - more
    return np.array(counts)


def bell_draw(rng, dims, scale, bound, split=(), held_as=jnp.bfloat16):
    loudness = block_scale(rng, dims, split, -0.22, 0.18) if split else 1.0
    drawn = jax.random.normal(rng, dims, jnp.float32) * scale * loudness
    return jnp.minimum(jnp.maximum(drawn, -bound), bound).astype(held_as)


def setup_inputs(seed: int = 0) -> dict:
    streams_of = jax.random.split(jax.random.key(seed), 11)
    fwd_now = draw_fwd_now(jax.random.fold_in(streams_of[10], 71), 0)
    fwd_prev = draw_fwd_prev(jax.random.fold_in(streams_of[10], 71), 0)
    adj_now = draw_adj_now(jax.random.fold_in(streams_of[10], 71), 0)
    adj_prev = draw_adj_prev(jax.random.fold_in(streams_of[10], 71), 0)
    shear_mod = jnp.clip(jnp.exp(math.log(2.0) - 1.3862944 * jax.random.uniform(streams_of[4], (NODES, ELEMENTS), jnp.float32) ** block_scale(streams_of[4], (NODES, ELEMENTS), ((1, 32),), -0.2, 0.2)), 0.5, 2.0)
    density = jnp.clip(jnp.exp(math.log(2.0) - 1.3862944 * jax.random.uniform(streams_of[5], (ELEMENTS,), jnp.float32) ** block_scale(streams_of[5], (ELEMENTS,), ((0, 32),), -0.2, 0.2)), 0.5, 2.0)
    station_owner_keys = jax.random.split(jax.random.fold_in(streams_of[6], 1), STATIONS // ST_DEV)
    station_owner_turns = jax.random.permutation(jax.random.fold_in(streams_of[6], 3), STATIONS // ST_DEV)
    station_owner = jax.vmap(lambda own, number: deal_out(jax.random.fold_in(streams_of[6], 2), own, number, ST_DEV, N_SPACE, 1, CAP, 2))(station_owner_keys, station_owner_turns).reshape((STATIONS, 1))
    receiver_local = plant(jax.random.randint(streams_of[7], (STATIONS,), 0, ELEM_DEV), jax.random.fold_in(streams_of[7], 1), 0, ELEM_DEV - 1).astype(jnp.int32)
    station_weights = bell_draw(streams_of[8], (NODES, STATIONS), 1.0, 6.0, ((1, 32),), jnp.float32)
    adj_records = bell_draw(streams_of[9], (EVENTS, STEPS, STATIONS), 1.0, 6.0, ((0, 8), (2, 32)), jnp.float32)
    return {"fwd_now": fwd_now, "fwd_prev": fwd_prev, "adj_now": adj_now, "adj_prev": adj_prev, "shear_mod": shear_mod, "density": density, "station_owner": station_owner, "receiver_local": receiver_local, "station_weights": station_weights, "adj_records": adj_records}


TIME_STEP = 0.08
STEP_SQUARE = 0.0064

def element_tables():
    root = 1.0 / np.sqrt(5.0)
    points = np.array([-1.0, -root, root, 1.0])
    weights = np.array([1.0 / 6.0, 5.0 / 6.0, 5.0 / 6.0, 1.0 / 6.0])
    derivative = np.zeros((4, 4))
    for i in range(4):
        for j in range(4):
            if i == j:
                derivative[i, i] = sum((1.0 / (points[i] - points[k]) for k in range(4) if k != i))
            else:
                upper = 1.0
                for k in range(4):
                    if k != i and k != j:
                        upper = upper * (points[i] - points[k])
                lower = 1.0
                for k in range(4):
                    if k != j:
                        lower = lower * (points[j] - points[k])
                derivative[i, j] = upper / lower
    identity = np.eye(4)
    grad_a = np.kron(np.eye(16), derivative)
    grad_b = np.kron(identity, np.kron(derivative, identity))
    grad_c = np.kron(derivative, np.eye(16))
    weight3 = np.kron(weights, np.kron(weights, weights))
    return (jnp.asarray(np.stack([grad_a, grad_b, grad_c]), jnp.float32), jnp.asarray(weight3, jnp.float32))

def shifted(values, offset, keep):
    filler = jnp.zeros_like(values[..., :abs(offset)])
    if offset > 0:
        moved = jnp.concatenate([values[..., offset:], filler], axis=-1)
    else:
        moved = jnp.concatenate([filler, values[..., :offset]], axis=-1)
    return jnp.where(keep, moved, jnp.zeros_like(moved))

def assemble_axis(grid, axis, stride, first, last):
    low = jnp.take(grid, 0, axis=axis)
    high = jnp.take(grid, 3, axis=axis)
    new_low = low + shifted(high, -stride, jnp.logical_not(first))
    new_high = high + shifted(low, stride, jnp.logical_not(last))
    middle = lax.slice_in_dim(grid, 1, 3, axis=axis)
    return jnp.concatenate([jnp.expand_dims(new_low, axis), middle, jnp.expand_dims(new_high, axis)], axis=axis)

def assemble(field):
    count = field.shape[0]
    elements = field.shape[-1]
    cells = EX * EY
    depth = elements // cells
    element = jnp.arange(elements, dtype=jnp.int32)
    col_x = element % EX
    col_y = element // EX % EY
    col_z = element // cells
    grid = field.reshape(count, 4, 4, 4, elements)
    grid = assemble_axis(grid, 3, 1, col_x == 0, col_x == EX - 1)
    grid = assemble_axis(grid, 2, EX, col_y == 0, col_y == EY - 1)
    grid = assemble_axis(grid, 1, cells, col_z == 0, col_z == depth - 1)
    return grid.reshape(count, 64, elements)

def reference(fwd_now, fwd_prev, adj_now, adj_prev, shear_mod, density, station_owner, receiver_local, station_weights, adj_records):
    grad_ops, weight3 = element_tables()
    elements = fwd_now.shape[-1]
    stiff = weight3[:, None] * shear_mod
    mass = assemble((weight3[:, None] * density[None, :])[None])[0]
    global_elem = (station_owner[:, 0] * (EX * EY * LAYERS) + receiver_local).astype(jnp.int32)
    high = lax.Precision.HIGHEST

    def per_event(kern, inputs):
        fwd_a, fwd_b, adj_a, adj_b, record = inputs
        source = jnp.zeros((STEPS, 64, elements), jnp.float32).at[:, :, global_elem].add(record[:, None, :] * station_weights[None, :, :])
        now = jnp.stack([fwd_a, adj_a])
        before = jnp.stack([fwd_b, adj_b])
        for step in range(STEPS):
            grads = jnp.einsum('dnm,fme->dfne', grad_ops, now, precision=high)
            kern = kern - TIME_STEP * stiff * lax.optimization_barrier(jnp.sum(grads[:, 0] * grads[:, 1], axis=0))
            local = jnp.einsum('dnm,dfne->fme', grad_ops, grads * stiff[None, None], precision=high)
            local = local - jnp.stack([jnp.zeros_like(source[step]), source[step]])
            after = 2.0 * now - before - STEP_SQUARE * assemble(local) / mass[None]
            before = now
            now = after
        return (kern, (now[0], before[0], now[1], before[1]))
    kern, outs = lax.scan(per_event, jnp.zeros((64, elements), jnp.float32), (fwd_now, fwd_prev, adj_now, adj_prev, adj_records))
    return (outs[0], outs[1], outs[2], outs[3], kern)
```

```python
import jax
import jax.numpy as jnp
import numpy as np
from jax import lax
from jax.experimental import pallas as pl
from jax.experimental.pallas import tpu as pltpu
from jax.sharding import PartitionSpec as P

MESH = pl.DeviceIdType.MESH
DMA = pltpu.SemaphoreType.DMA
VM = pl.BlockSpec(memory_space=pltpu.VMEM)
F32 = jnp.float32
SLABS, EVENT, CAP, ST, ELEMS = 32, 8, 256, 2048, 1024
DIRECT = 32
TIME_STEP, STEP_SQUARE = 0.08, 0.0064


def derivative_table():
    root = 1.0 / np.sqrt(5.0)
    p = np.array([-1.0, -root, root, 1.0])
    d = np.zeros((4, 4))
    for i in range(4):
        for j in range(4):
            if i == j:
                d[i, i] = sum(1.0 / (p[i] - p[k]) for k in range(4) if k != i)
            else:
                upper = np.prod([p[i] - p[k] for k in range(4) if k not in (i, j)])
                lower = np.prod([p[j] - p[k] for k in range(4) if k != j])
                d[i, j] = upper / lower
    return d


D = derivative_table()
ALPHA, BETA = float((D[0, 0] + D[0, 3]) / 2), float((D[1, 0] + D[1, 3]) / 2)
B00, B01 = float((D[0, 0] - D[0, 3]) / 2), float((D[0, 1] - D[0, 2]) / 2)
B10, B11 = float((D[1, 0] - D[1, 3]) / 2), float((D[1, 1] - D[1, 2]) / 2)


def gradient(f):
    e, o0, o1 = (f[0] + f[3]) - (f[1] + f[2]), f[0] - f[3], f[1] - f[2]
    a0, a1 = ALPHA * e, BETA * e
    b0, b1 = B00 * o0 + B01 * o1, B10 * o0 + B11 * o1
    return [b0 + a0, b1 + a1, b1 - a1, b0 - a0]


def divergence(t):
    e0, e1, o0, o1 = t[0] + t[3], t[1] + t[2], t[0] - t[3], t[1] - t[2]
    r = ALPHA * o0 + BETA * o1
    q0, q1 = B00 * e0 + B10 * e1, B01 * e0 + B11 * e1
    return [r + q0, q1 - r, -q1 - r, r - q0]


def node_weight(n):
    def w(i):
        return jnp.where((i == 0) | (i == 3), np.float32(1.0 / 6.0), np.float32(5.0 / 6.0))

    return w(n % 4) * w(n // 4 % 4) * w(n // 16)


def coords():
    me, ev = lax.axis_index("space"), lax.axis_index("event")
    return me, ev, me // 8, me // 2 % 4, me % 2, ev // 2, ev % 2


def copy_to(src, dst, send, recv, **where):
    return pltpu.make_async_remote_copy(
        src_ref=src, dst_ref=dst, send_sem=send, recv_sem=recv, device_id=where, device_id_type=MESH
    )


def signal(barrier, inc=1, **where):
    pl.semaphore_signal(barrier, inc=inc, device_id=where, device_id_type=MESH)


def place_kernel(owner, ids, weights, records, send_w, send_r, tail, rows, placed, spots_v, spots, sem):
    x = lax.axis_index("event") // 2
    slab = lax.broadcasted_iota(jnp.int32, (SLABS, 256), 0)
    earlier = (
        lax.broadcasted_iota(jnp.int32, (256, 256), 0) < lax.broadcasted_iota(jnp.int32, (256, 256), 1)
    ).astype(F32).astype(jnp.bfloat16)
    named = [jnp.where(owner[b : b + 1, :] == slab, 1.0, 0.0).astype(F32) for b in range(8)]
    counts = jnp.dot(
        jnp.concatenate(named, axis=0).astype(jnp.bfloat16), earlier, preferred_element_type=F32
    )
    carry = jnp.zeros((SLABS, 1), F32)
    for b in range(8):
        rank = jnp.sum(named[b] * (counts[32 * b : 32 * b + 32] + carry), axis=0, keepdims=True)
        carry = carry + jnp.sum(named[b], axis=1, keepdims=True)
        spots_v[b : b + 1, :] = owner[b : b + 1, :] * CAP + rank.astype(jnp.int32)
    copy = pltpu.make_async_copy(spots_v, spots, sem)
    copy.start()
    tail[...] = jnp.zeros_like(tail)
    for k in range(4):
        tail[k : k + 1, :] = records[k // 2, k % 2 : k % 2 + 1, :]
    tail[4:5, :] = ids[...].astype(F32)
    for c in range(ST // 128):
        cols = slice(128 * c, 128 * c + 128)
        block = jnp.concatenate(
            [weights[pl.ds(pl.multiple_of((x + q) % 4 * 16, 16), 16), cols] for q in range(DIRECT // 16)]
            + [tail[:, cols], jnp.zeros((120 - DIRECT, 128), F32)],
            axis=0,
        )
        rows[cols, :] = block.T

    def clear(i, carry):
        placed[pl.ds(pl.multiple_of(i * 128, 128), 128), :] = jnp.zeros((128, 128), F32)
        return carry

    lax.fori_loop(0, SLABS * CAP // 128, clear, 0)
    copy.wait()

    def move(i, carry):
        for j in range(16):
            spot = spots[i // 16, i % 16 * 16 + j]
            placed[pl.ds(spot, 1), :] = rows[pl.ds(i * 16 + j, 1), :]
        return carry

    lax.fori_loop(0, ST // 16, move, 0)

    def turn(t, carry):
        for h in range(2):
            block = placed[pl.ds(pl.multiple_of(t * CAP + h * 128, 128), 128), :].T
            send_w[t, :, 128 * h : 128 * h + 128] = block[:DIRECT]
            for r in range(5):
                send_r[t, :, 256 * r + 128 * h : 256 * r + 128 * h + 128] = block[DIRECT + r : DIRECT + r + 1]
        return carry

    lax.fori_loop(0, SLABS, turn, 0)


def place(owner, ids, weights, records):
    return pl.pallas_call(
        place_kernel,
        out_shape=(
            jax.ShapeDtypeStruct((SLABS, DIRECT, CAP), F32),
            jax.ShapeDtypeStruct((SLABS, 1, 5 * CAP), F32),
        ),
        in_specs=[VM] * 4,
        out_specs=(VM, VM),
        scratch_shapes=[
            pltpu.VMEM((8, ST), F32),
            pltpu.VMEM((ST, 128), F32),
            pltpu.VMEM((SLABS * CAP, 128), F32),
            pltpu.VMEM((8, 256), jnp.int32),
            pltpu.SMEM((8, 256), jnp.int32),
            DMA,
        ],
        compiler_params=pltpu.CompilerParams(vmem_limit_bytes=40 << 20),
        name="place",
    )(owner, ids, weights, records)


def weight_goal(dy, dz):
    me, ev, y, z, c, x, half = coords()
    deep = half * 4 + z
    step = (0, 1, 7)[dz] if dz < 3 else 2 + 4 * ((deep // 2 + dy) % 2)
    deep = (deep + step) % 8
    return (y + dy) % 4 * 8 + deep % 4 * 2, x * 2 + deep // 4


def record_goal(dy, dz):
    me, ev, y, z, c, x, half = coords()
    return (y + dy) % 4 * 8 + (z + (0, 1, 3, 2)[dz]) % 4 * 2


def greet_stations(barrier):
    me, ev, y, z, c, x, half = coords()
    for dy in range(4):
        for dz in range(4):
            if dy == 0 and dz == 0:
                signal(barrier, 2, space=me + 1 - 2 * c)
                continue
            goal, event = weight_goal(dy, dz)
            other = record_goal(dy, dz)
            for c2 in range(2):
                signal(barrier, space=goal + c2, event=event)
                signal(barrier, space=other + c2)
    signal(barrier, event=(ev + 2) % 8)
    signal(barrier, event=(ev + 6) % 8)
    return 64


def send_stations(send_w, send_r, got_w, got_r, sw, rw, sr, rr):
    me, ev, y, z, c, x, half = coords()
    here = (0, 0, c)
    own = [
        pltpu.make_async_copy(send_w.at[me], got_w.at[here], rw.at[here]),
        pltpu.make_async_copy(send_r.at[me], got_r.at[here], rr.at[here]),
    ]
    for copy in own:
        copy.start()
    copies = []
    for dy in range(4):
        for dz in range(4):
            for c2 in range(2):
                if dy == 0 and dz == 0:
                    if c2 == 0:
                        continue
                    goal = other = me + 1 - 2 * c
                    event = ev
                else:
                    goal, event = weight_goal(dy, dz)
                    goal, other = goal + c2, record_goal(dy, dz) + c2
                mine, there = (dy, dz, c2), (dy, dz, c)
                copies += [
                    copy_to(send_w.at[goal], got_w.at[there], sw.at[mine], rw.at[there], space=goal, event=event),
                    copy_to(send_r.at[other], got_r.at[there], sr.at[mine], rr.at[there], space=other),
                ]
                copies[-2].start()
                copies[-1].start()
    return copies


def gather_sources(got_w, got_r, left, right, left_part, onehot, total, rw, rr, fs, fr):
    me, ev, y, z, c, x, half = coords()

    def shares(w):
        return (
            copy_to(got_w.at[w, :, :, 0:16], left.at[w], fs.at[w, 0], fr.at[w, 0], event=(ev + 2) % 8),
            copy_to(got_w.at[w, :, :, 16:32], right.at[w], fs.at[w, 1], fr.at[w, 1], event=(ev + 6) % 8),
        )

    def receive(w):
        for dz in range(4):
            for cs in range(2):
                at = (w, dz, cs)
                pltpu.make_async_copy(got_w.at[at], got_w.at[at], rw.at[at]).wait()
                pltpu.make_async_copy(got_r.at[at], got_r.at[at], rr.at[at]).wait()
        for copy in shares(w):
            copy.start()

    def add(w, carry):
        @pl.when(w < 3)
        def _():
            receive(w + 1)

        for copy in shares(w):
            copy.wait_recv()

        def block(k, carry):
            at = (w, k // 2, k % 2)
            cols = pl.ds(pl.multiple_of(k * CAP, CAP), CAP)
            nodes = jnp.concatenate([got_w[at], right[at], left[at]], axis=0)
            samples = got_r[at]
            for q in range(4):
                product = nodes * samples[:, 256 * q : 256 * q + 256]
                upper = product.astype(jnp.bfloat16)
                left_part[64 * q : 64 * q + 64, cols] = upper
                left_part[256 + 64 * q : 320 + 64 * q, cols] = (product - upper.astype(F32)).astype(jnp.bfloat16)
            spot = samples[:, 1024:1280].astype(jnp.int32)
            for i in range(8):
                row = lax.broadcasted_iota(jnp.int32, (128, CAP), 0) + 128 * i
                onehot[128 * i : 128 * i + 128, cols] = jnp.where(row == spot, 1.0, 0.0).astype(jnp.bfloat16)
            return carry

        lax.fori_loop(0, 8, block, 0)

        def columns(j, carry):
            at = pl.ds(pl.multiple_of(j * 256, 256), 256)
            total[j] = total[j] + lax.dot_general(
                left_part[...], onehot[at, :], (((1,), (1,)), ((), ())), preferred_element_type=F32
            )
            return carry

        lax.fori_loop(0, 4, columns, 0)
        return carry

    total[...] = jnp.zeros_like(total)
    receive(0)
    lax.fori_loop(0, 4, add, 0)


def spread_sources(total, src):
    x = lax.axis_index("event") // 2

    def tile(i, carry):
        q, r = i // 8, i % 8
        goal = q * 8 + (r // 2 + x) % 4 * 2 + r % 2
        for j in range(8):
            cols = slice(j % 2 * 128, j % 2 * 128 + 128)
            upper = total[j // 2, pl.ds(pl.multiple_of(i * 8, 8), 8), cols]
            lower = total[j // 2, pl.ds(pl.multiple_of(256 + i * 8, 8), 8), cols]
            src[pl.ds(pl.multiple_of(goal * 64 + j * 8, 8), 8), :] = upper + lower
        return carry

    lax.fori_loop(0, 32, tile, 0)


def row_of(n):
    return n // 8 * 64 + n % 8


def strided(base):
    return pl.ds(base, 8, stride=8)


def tile_of(n):
    return pl.ds(pl.multiple_of(n * 8, 8), 8)


def element_masks():
    sub = lax.broadcasted_iota(jnp.int32, (8, 128), 0)
    lane = lax.broadcasted_iota(jnp.int32, (8, 128), 1)
    return sub, lane


def from_before_x(v):
    sub, lane = element_masks()
    return jnp.where(lane % 16 != 0, pltpu.roll(v, 1, 1), 0.0)


def from_before_y(v):
    sub, lane = element_masks()
    turned = pltpu.roll(v, 16, 1)
    moved = jnp.where(lane < 16, pltpu.roll(turned, 1, 0), turned)
    return jnp.where((sub % 2 != 0) | (lane >= 16), moved, 0.0)


def after_x(v, old):
    sub, lane = element_masks()
    return jnp.where(lane % 16 != 15, pltpu.roll(v, 127, 1), old)


def after_y(v, old):
    sub, lane = element_masks()
    turned = pltpu.roll(v, 112, 1)
    moved = jnp.where(lane >= 112, pltpu.roll(turned, 7, 0), turned)
    return jnp.where((sub % 2 != 1) | (lane < 112), moved, old)


def stiffness(now, local, stiff, terms, first):
    def line(nodes, fresh, fresh_terms):
        mu = [stiff[n] for n in nodes]
        sums = [None] * 4
        for e in range(2):
            g = []
            for f in (e, e + 2):
                grad = gradient([now[f * 64 + n] for n in nodes])
                out = divergence([a * b for a, b in zip(grad, mu)])
                for n, value in zip(nodes, out):
                    local[f * 64 + n] = value if fresh else local[f * 64 + n] + value
                g.append(grad)
            for i in range(4):
                pair = g[0][i] * g[1][i]
                sums[i] = pair if e == 0 else sums[i] + pair
        for n, value in zip(nodes, sums):
            terms[tile_of(n), :] = value if fresh_terms else terms[tile_of(n), :] + value

    def along_a(l, carry):
        line([4 * l + i for i in range(4)], True, first)
        return carry

    def along_b(l, carry):
        line([l // 4 * 16 + l % 4 + 4 * i for i in range(4)], False, False)
        return carry

    def along_c(l, carry):
        line([l + 16 * i for i in range(4)], False, False)
        return carry

    for body in (along_a, along_b, along_c):
        lax.fori_loop(0, 16, body, 0)


def assemble_xy(local, first, count):
    def along_x(l, carry):
        at = first * 64 + 4 * l
        low, high = local[at], local[at + 3]
        new = low + from_before_x(high)
        local[at] = new
        local[at + 3] = after_x(new, high)
        return carry

    def along_y(l, carry):
        at = first * 64 + l // 4 * 16 + l % 4
        low, high = local[at], local[at + 12]
        new = low + from_before_y(high)
        local[at] = new
        local[at + 12] = after_y(new, high)
        return carry

    lax.fori_loop(0, 16 * count, along_x, 0)
    lax.fori_loop(0, 16 * count, along_y, 0)


def pack_faces(local, faces):
    sub, lane = element_masks()

    def group(i, carry):
        base = i // 4 * 64 + i % 4 * 4
        low = local[base]
        high = pltpu.roll(local[base + 48], 2, 0)
        for q in range(1, 4):
            low = jnp.where(sub // 2 == q, pltpu.roll(local[base + q], 2 * q, 0), low)
            high = jnp.where(sub // 2 == q, pltpu.roll(local[base + 48 + q], (2 * q + 2) % 8, 0), high)
        faces[0, i] = low
        faces[1, i] = high
        return carry

    lax.fori_loop(0, 16, group, 0)


def assemble_z(local, got):
    me = lax.axis_index("space")
    sub, lane = element_masks()

    def group(i, carry):
        base = i // 4 * 64 + i % 4 * 4
        before = jnp.where(me > 0, got[0, i], 0.0)
        after = jnp.where(me < SLABS - 1, got[1, i], 0.0)
        for q in range(4):
            low, high = local[base + q], local[base + 48 + q]
            mine = pltpu.roll(before, (8 - 2 * q) % 8, 0) if q else before
            new = low + jnp.where(sub < 2, mine, pltpu.roll(high, 2, 0))
            theirs = pltpu.roll(after, (6 - 2 * q) % 8, 0) if q < 3 else after
            local[base + q] = new
            local[base + 48 + q] = jnp.where(sub < 6, pltpu.roll(new, 6, 0), high + theirs)
        return carry

    lax.fori_loop(0, 16, group, 0)


def inverse_mass(density, got, table, inv):
    me = lax.axis_index("space")
    sub, lane = element_masks()

    def planes(v):
        out = []
        low = v + from_before_x(v)
        for a in (low, v, after_x(low, v)):
            new = a + from_before_y(a)
            out += [(new, a, after_y(new, a))]
        return out

    here = planes(density)
    before = planes(jnp.where(me > 0, got[0], 0.0))
    after = planes(jnp.where(me < SLABS - 1, got[1], 0.0))
    for a in range(3):
        for b in range(3):
            v = here[a][b]
            low = v + jnp.where(sub < 2, pltpu.roll(before[a][b], 2, 0), pltpu.roll(v, 2, 0))
            high = v + jnp.where(sub < 6, pltpu.roll(v, 6, 0), pltpu.roll(after[a][b], 6, 0))
            for c, value in enumerate((low, v, high)):
                table[9 * c + 3 * b + a] = 1.0 / value

    def node(n, carry):
        def part(i):
            return (i + 1) // 2

        at = part(n // 16) * 9 + part(n // 4 % 4) * 3 + part(n % 4)
        inv[n] = table[at] * (np.float32(STEP_SQUARE) / node_weight(n))
        return carry

    lax.fori_loop(0, 64, node, 0)


def step_kernel(
    send_w, send_r, fwd_now, fwd_prev, adj_now, adj_prev, shear, density,
    one, two, pieces,
    got_w, got_r, left, right, left_part, onehot, total, src,
    zero, local, stiff, inv, table, terms, faces, got_faces, got_density, out_terms,
    sw, rw, sr, rr, fs, fr, hs, hr, ds, dr, ts, tr,
):
    me, ev, y, z, c, x, half = coords()
    up, down = (me + 1) % SLABS, (me + SLABS - 1) % SLABS
    barrier = pltpu.get_barrier_semaphore()
    greeted = greet_stations(barrier)
    for k in range(1, EVENT):
        signal(barrier, event=(ev + k) % EVENT)
    signal(barrier, space=up)
    signal(barrier, space=down)

    def load(n, carry):
        for f, ref in enumerate((fwd_now, adj_now)):
            for e in range(2):
                zero[(2 * f + e) * 64 + n] = ref[strided(e * 512 + row_of(n)), :]
        stiff[n] = shear[strided(row_of(n)), :] * node_weight(n)
        return carry

    lax.fori_loop(0, 64, load, 0)
    pl.semaphore_wait(barrier, greeted + EVENT - 1 + 2)

    copies = send_stations(send_w, send_r, got_w, got_r, sw, rw, sr, rr)
    weigh = [
        copy_to(density, got_density.at[1], ds.at[1], dr.at[1], space=down),
        copy_to(density, got_density.at[0], ds.at[0], dr.at[0], space=up),
    ]
    for copy in weigh:
        copy.start()

    stiffness(zero, local, stiff, terms, True)
    assemble_xy(local, 0, 2)
    for copy in weigh:
        copy.wait()
    inverse_mass(density[...], got_density, table, inv)

    gather_sources(got_w, got_r, left, right, left_part, onehot, total, rw, rr, fs, fr)
    spread_sources(total, src)

    now, later = zero, one
    for step in range(2):
        def less(n, carry):
            for e in range(2):
                at = (2 + e) * 64 + n
                local[at] = local[at] - src[strided((2 * e + step) * 512 + row_of(n)), :]
            return carry

        lax.fori_loop(0, 64, less, 0)
        if step == 0:
            assemble_xy(local, 2, 2)
        else:
            assemble_xy(local, 0, 4)
        pack_faces(local, faces.at[step])
        halo = [
            copy_to(faces.at[step, 0], got_faces.at[step, 1], hs.at[step, 0], hr.at[step, 0], space=down),
            copy_to(faces.at[step, 1], got_faces.at[step, 0], hs.at[step, 1], hr.at[step, 1], space=up),
        ]
        for copy in halo:
            copy.start()
        copies += halo
        for copy in halo:
            copy.wait_recv()
        assemble_z(local, got_faces.at[step])

        def update(n, carry):
            mine = inv[n]
            for f in range(4):
                at = f * 64 + n
                if step == 0:
                    old = (fwd_prev, adj_prev)[f // 2][strided(f % 2 * 512 + row_of(n)), :]
                else:
                    old = zero[at]
                later[at] = 2.0 * now[at] - old - local[at] * mine
            return carry

        lax.fori_loop(0, 64, update, 0)
        if step == 0:
            stiffness(one, local, stiff, terms, False)
            now, later = one, two

            def cut(j, carry):
                out_terms[j] = terms[pl.ds(j, 64, stride=8), :]
                return carry

            lax.fori_loop(0, EVENT, cut, 0)
            for k in range(1, EVENT):
                goal = (ev + k) % EVENT
                copies.append(copy_to(out_terms.at[goal], pieces.at[k], ts.at[k], tr.at[k], event=goal))
                copies[-1].start()
            pieces[0] = out_terms[ev]

    for copy in copies[-9:-2]:
        copy.wait_recv()
    for copy in copies:
        copy.wait_send()

    def last(w, carry):
        copy_to(got_w.at[w, :, :, 0:16], left.at[w], fs.at[w, 0], fr.at[w, 0], event=(ev + 2) % 8).wait_send()
        copy_to(got_w.at[w, :, :, 16:32], right.at[w], fs.at[w, 1], fr.at[w, 1], event=(ev + 6) % 8).wait_send()
        return carry

    lax.fori_loop(0, 4, last, 0)


def steps(send_w, send_r, fwd_now, fwd_prev, adj_now, adj_prev, shear, density):
    fields = pltpu.VMEM((256, 8, 128), F32)
    waves = DMA((4, 4, 2))
    return pl.pallas_call(
        step_kernel,
        out_shape=(
            jax.ShapeDtypeStruct((256, 8, 128), F32),
            jax.ShapeDtypeStruct((256, 8, 128), F32),
            jax.ShapeDtypeStruct((EVENT, 64, 128), F32),
        ),
        in_specs=[VM] * 8,
        out_specs=(VM, VM, VM),
        scratch_shapes=[
            pltpu.VMEM((4, 4, 2, DIRECT, CAP), F32),
            pltpu.VMEM((4, 4, 2, 1, 5 * CAP), F32),
            pltpu.VMEM((4, 4, 2, 16, CAP), F32),
            pltpu.VMEM((4, 4, 2, 16, CAP), F32),
            pltpu.VMEM((512, 8 * CAP), jnp.bfloat16),
            pltpu.VMEM((ELEMS, 8 * CAP), jnp.bfloat16),
            pltpu.VMEM((4, 512, 256), F32),
            pltpu.VMEM((2048, 128), F32),
            fields,
            fields,
            pltpu.VMEM((64, 8, 128), F32),
            pltpu.VMEM((64, 8, 128), F32),
            pltpu.VMEM((27, 8, 128), F32),
            pltpu.VMEM((512, 128), F32),
            pltpu.VMEM((2, 2, 16, 8, 128), F32),
            pltpu.VMEM((2, 2, 16, 8, 128), F32),
            pltpu.VMEM((2, 8, 128), F32),
            pltpu.VMEM((EVENT, 64, 128), F32),
            waves, waves, waves, waves,
            DMA((4, 2)), DMA((4, 2)),
            DMA((2, 2)), DMA((2, 2)),
            DMA((2,)), DMA((2,)),
            DMA((EVENT,)), DMA((EVENT,)),
        ],
        compiler_params=pltpu.CompilerParams(collective_id=0, has_side_effects=True, vmem_limit_bytes=56 << 20),
        name="steps",
    )(send_w, send_r, fwd_now, fwd_prev, adj_now, adj_prev, shear, density)


def finish_kernel(one, two, pieces, shear, fwd_last, fwd_before, adj_last, adj_before, kernel):
    ev = lax.axis_index("event")

    def node(n, carry):
        for f in range(4):
            last, before = ((fwd_last, fwd_before), (adj_last, adj_before))[f // 2]
            at = strided(f % 2 * 512 + row_of(n))
            before[at, :] = one[f * 64 + n]
            last[at, :] = two[f * 64 + n]
        return carry

    lax.fori_loop(0, 64, node, 0)
    for b in range(8):
        rows = slice(8 * b, 8 * b + 8)
        total = pieces[0, rows]
        for k in range(1, EVENT):
            total = total + pieces[k, rows]
        n = 8 * b + lax.broadcasted_iota(jnp.int32, (8, 128), 0)
        factor = node_weight(n) * np.float32(-TIME_STEP)
        kernel[rows, :] = total * (factor * shear[pl.ds(pl.multiple_of(b * 64 + ev * 8, 8), 8), :])


def finish(one, two, pieces, shear):
    return pl.pallas_call(
        finish_kernel,
        out_shape=(*[jax.ShapeDtypeStruct((1024, 128), F32)] * 4, jax.ShapeDtypeStruct((64, 128), F32)),
        in_specs=[VM] * 4,
        out_specs=(VM,) * 5,
        compiler_params=pltpu.CompilerParams(vmem_limit_bytes=30 << 20),
        name="finish",
    )(one, two, pieces, shear)


def to_rows(field):
    count = field.size // (64 * ELEMS)
    return field.reshape(count, 8, 8, 8, 128).transpose(0, 1, 3, 2, 4).reshape(count * 512, 128)


def from_rows(rows):
    return rows.reshape(2, 8, 8, 8, 128).transpose(0, 1, 3, 2, 4).reshape(2, 64, ELEMS)


def shards(
    fwd_now, fwd_prev, adj_now, adj_prev, shear_mod, density, station_owner, receiver_local, station_weights, adj_records
):
    shear = to_rows(shear_mod)
    send_w, send_r = place(
        station_owner.reshape(8, 256), receiver_local.reshape(1, ST), station_weights, adj_records
    )
    one, two, pieces = steps(
        send_w, send_r, to_rows(fwd_now), to_rows(fwd_prev), to_rows(adj_now), to_rows(adj_prev),
        shear, density.reshape(8, 128),
    )
    *fields, kernel = finish(one, two, pieces, shear)
    return (*map(from_rows, fields), kernel)


def solution(mesh):
    fields = P("event", None, "space")
    return jax.shard_map(
        shards,
        mesh=mesh,
        in_specs=(
            fields, fields, fields, fields,
            P(None, "space"), P("space"), P("space", None), P("space"), P(None, "space"), fields,
        ),
        out_specs=(fields, fields, fields, fields, P(None, ("space", "event"))),
        check_vma=False,
    )
```

```python
import jax
import jax.numpy as jnp
import numpy as np
from jax import lax
from jax.experimental import pallas as pl
from jax.experimental.pallas import tpu as pltpu
from jax.sharding import PartitionSpec as P

MESH = pl.DeviceIdType.MESH
DMA = pltpu.SemaphoreType.DMA
VM = pl.BlockSpec(memory_space=pltpu.VMEM)
HBM = pl.BlockSpec(memory_space=pltpu.HBM)
F32 = jnp.float32
SLABS, EVENT, CAP, ST, ELEMS = 32, 8, 256, 2048, 1024
DIRECT = 32
TIME_STEP, STEP_SQUARE = 0.08, 0.0064


def derivative_table():
    root = 1.0 / np.sqrt(5.0)
    p = np.array([-1.0, -root, root, 1.0])
    d = np.zeros((4, 4))
    for i in range(4):
        for j in range(4):
            if i == j:
                d[i, i] = sum(1.0 / (p[i] - p[k]) for k in range(4) if k != i)
            else:
                upper = np.prod([p[i] - p[k] for k in range(4) if k not in (i, j)])
                lower = np.prod([p[j] - p[k] for k in range(4) if k != j])
                d[i, j] = upper / lower
    return d


D = derivative_table()
ALPHA, BETA = float((D[0, 0] + D[0, 3]) / 2), float((D[1, 0] + D[1, 3]) / 2)
B00, B01 = float((D[0, 0] - D[0, 3]) / 2), float((D[0, 1] - D[0, 2]) / 2)
B10, B11 = float((D[1, 0] - D[1, 3]) / 2), float((D[1, 1] - D[1, 2]) / 2)


def gradient(f):
    e, o0, o1 = (f[0] + f[3]) - (f[1] + f[2]), f[0] - f[3], f[1] - f[2]
    a0, a1 = ALPHA * e, BETA * e
    b0, b1 = B00 * o0 + B01 * o1, B10 * o0 + B11 * o1
    return [b0 + a0, b1 + a1, b1 - a1, b0 - a0]


def divergence(t):
    e0, e1, o0, o1 = t[0] + t[3], t[1] + t[2], t[0] - t[3], t[1] - t[2]
    r = ALPHA * o0 + BETA * o1
    q0, q1 = B00 * e0 + B10 * e1, B01 * e0 + B11 * e1
    return [r + q0, q1 - r, -q1 - r, r - q0]


def node_weight(n):
    def w(i):
        return jnp.where((i == 0) | (i == 3), np.float32(1.0 / 6.0), np.float32(5.0 / 6.0))

    return w(n % 4) * w(n // 4 % 4) * w(n // 16)


def inverse_weight(n):
    def w(i):
        return jnp.where((i == 0) | (i == 3), np.float32(6.0), np.float32(1.2))

    return w(n % 4) * w(n // 4 % 4) * w(n // 16)


def coords():
    me, ev = lax.axis_index("space"), lax.axis_index("event")
    return me, ev, me // 8, me // 2 % 4, me % 2, ev // 2, ev % 2


def copy_to(src, dst, send, recv, **where):
    return pltpu.make_async_remote_copy(
        src_ref=src, dst_ref=dst, send_sem=send, recv_sem=recv, device_id=where, device_id_type=MESH
    )


def signal(barrier, inc=1, **where):
    pl.semaphore_signal(barrier, inc=inc, device_id=where, device_id_type=MESH)


def place_kernel(
    owner_h, ids_h, weights_h, records_h, send_w, send_r,
    owner, ids, weights, records, tail, rows, placed, spots_v, spots, sem, ins,
):
    x = lax.axis_index("event") // 2
    fetch = [
        pltpu.make_async_copy(a, b, ins.at[k])
        for k, (a, b) in enumerate(((owner_h, owner), (ids_h, ids), (records_h, records), (weights_h, weights)))
    ]
    for copy in fetch:
        copy.start()
    fetch[0].wait()
    slab = lax.broadcasted_iota(jnp.int32, (SLABS, 256), 0)
    earlier = (
        lax.broadcasted_iota(jnp.int32, (256, 256), 0) < lax.broadcasted_iota(jnp.int32, (256, 256), 1)
    ).astype(F32).astype(jnp.bfloat16)
    named = [jnp.where(owner[:, 256 * b : 256 * b + 256] == slab, 1.0, 0.0).astype(F32) for b in range(8)]
    counts = jnp.dot(
        jnp.concatenate(named, axis=0).astype(jnp.bfloat16), earlier, preferred_element_type=F32
    )
    carry, found = jnp.zeros((SLABS, 1), F32), []
    for b in range(8):
        rank = jnp.sum(named[b] * (counts[32 * b : 32 * b + 32] + carry), axis=0, keepdims=True)
        carry = carry + jnp.sum(named[b], axis=1, keepdims=True)
        found.append(owner[:, 256 * b : 256 * b + 256] * CAP + rank.astype(jnp.int32))
    for b in range(4):
        spots_v[b : b + 1, :] = found[b] + found[b + 4] * 65536
    copy = pltpu.make_async_copy(spots_v, spots, sem)
    copy.start()
    for k in range(1, 4):
        fetch[k].wait()
    tail[...] = jnp.zeros_like(tail)
    for k in range(4):
        tail[k : k + 1, :] = records[k // 2, k % 2 : k % 2 + 1, :]
    tail[4:5, :] = ids[...].astype(F32)
    for c in range(ST // 128):
        cols = slice(128 * c, 128 * c + 128)
        block = jnp.concatenate(
            [weights[pl.ds(pl.multiple_of((x + q) % 4 * 16, 16), 16), cols] for q in range(DIRECT // 16)]
            + [tail[:, cols], jnp.zeros((120 - DIRECT, 128), F32)],
            axis=0,
        )
        rows[cols, :] = block.T

    def clear(i, carry):
        placed[pl.ds(pl.multiple_of(i * 128, 128), 128), :] = jnp.zeros((128, 128), F32)
        return carry

    lax.fori_loop(0, SLABS * CAP // 128, clear, 0)
    copy.wait()

    def move(i, carry):
        for j in range(16):
            pair = spots[i // 16, i % 16 * 16 + j]
            placed[pl.ds(pair & 65535, 1), :] = rows[pl.ds(i * 16 + j, 1), :]
            placed[pl.ds(pair >> 16, 1), :] = rows[pl.ds(ST // 2 + i * 16 + j, 1), :]
        return carry

    lax.fori_loop(0, ST // 32, move, 0)

    def turn(t, carry):
        for h in range(2):
            block = placed[pl.ds(pl.multiple_of(t * CAP + h * 128, 128), 128), :].T
            send_w[t, :, 128 * h : 128 * h + 128] = block[:DIRECT]
            for r in range(5):
                send_r[t, :, 256 * r + 128 * h : 256 * r + 128 * h + 128] = block[DIRECT + r : DIRECT + r + 1]
        return carry

    lax.fori_loop(0, SLABS, turn, 0)


def place(owner, ids, weights, records):
    return pl.pallas_call(
        place_kernel,
        out_shape=(
            jax.ShapeDtypeStruct((SLABS, DIRECT, CAP), F32),
            jax.ShapeDtypeStruct((SLABS, 1, 5 * CAP), F32),
        ),
        in_specs=[HBM] * 4,
        out_specs=(VM, VM),
        scratch_shapes=[
            pltpu.VMEM((1, ST), jnp.int32),
            pltpu.VMEM((1, ST), jnp.int32),
            pltpu.VMEM((64, ST), F32),
            pltpu.VMEM((2, 2, ST), F32),
            pltpu.VMEM((8, ST), F32),
            pltpu.VMEM((ST, 128), F32),
            pltpu.VMEM((SLABS * CAP, 128), F32),
            pltpu.VMEM((4, 256), jnp.int32),
            pltpu.SMEM((4, 256), jnp.int32),
            DMA,
            DMA((4,)),
        ],
        compiler_params=pltpu.CompilerParams(vmem_limit_bytes=12 << 20),
        name="place",
    )(owner, ids, weights, records)


def weight_goal(dy, dz):
    me, ev, y, z, c, x, half = coords()
    deep = half * 4 + z
    step = (0, 1, 7)[dz] if dz < 3 else 2 + 4 * ((deep // 2 + dy) % 2)
    deep = (deep + step) % 8
    return (y + dy) % 4 * 8 + deep % 4 * 2, x * 2 + deep // 4


def record_goal(dy, dz):
    me, ev, y, z, c, x, half = coords()
    return (y + dy) % 4 * 8 + (z + (0, 1, 3, 2)[dz]) % 4 * 2


def greet_stations(barrier):
    me, ev, y, z, c, x, half = coords()
    for dy in range(4):
        for dz in range(4):
            if dy == 0 and dz == 0:
                signal(barrier, 2, space=me + 1 - 2 * c)
                continue
            goal, event = weight_goal(dy, dz)
            other = record_goal(dy, dz)
            for c2 in range(2):
                signal(barrier, space=goal + c2, event=event)
                signal(barrier, space=other + c2)
    signal(barrier, event=(ev + 2) % 8)
    signal(barrier, event=(ev + 6) % 8)
    return 64


def own_stations(send_w, send_r, got_w, got_r, rw, rr):
    me, ev, y, z, c, x, half = coords()
    here = (0, 0, c)
    pltpu.make_async_copy(send_w.at[me], got_w.at[here], rw.at[here]).start()
    pltpu.make_async_copy(send_r.at[me], got_r.at[here], rr.at[here]).start()


def station_copies(dy, first, send_w, send_r, got_w, got_r, sw, rw, sr, rr):
    me, ev, y, z, c, x, half = coords()
    copies = []
    for dz in range(4):
        for c2 in range(2):
            if first and dz == 0:
                if c2 == 0:
                    continue
                goal = other = me + 1 - 2 * c
                event = ev
            else:
                goal, event = weight_goal(dy, dz)
                goal, other = goal + c2, record_goal(dy, dz) + c2
            mine, there = (dy, dz, c2), (dy, dz, c)
            copies += [
                copy_to(send_w.at[goal], got_w.at[there], sw.at[mine], rw.at[there], space=goal, event=event),
                copy_to(send_r.at[other], got_r.at[there], sr.at[mine], rr.at[there], space=other),
            ]
    return copies


def share_copies(w, got_w, left, right, fs, fr):
    ev = lax.axis_index("event")
    return (
        copy_to(got_w.at[w, :, :, 0:16], left.at[w], fs.at[w, 0], fr.at[w, 0], event=(ev + 2) % 8),
        copy_to(got_w.at[w, :, :, 16:32], right.at[w], fs.at[w, 1], fr.at[w, 1], event=(ev + 6) % 8),
    )


def receive_stations(w, got_w, got_r, left, right, rw, rr, fs, fr):
    for dz in range(4):
        for cs in range(2):
            at = (w, dz, cs)
            pltpu.make_async_copy(got_w.at[at], got_w.at[at], rw.at[at]).wait()
            pltpu.make_async_copy(got_r.at[at], got_r.at[at], rr.at[at]).wait()
    for copy in share_copies(w, got_w, left, right, fs, fr):
        copy.start()


def gather_sources(got_w, got_r, left, right, left_part, onehot, total, receive, start, between, shares):
    def add(w, carry):
        def products(nodes, row, samples, cols):
            for q in range(4):
                product = nodes * samples[:, 256 * q : 256 * q + 256]
                upper = product.astype(jnp.bfloat16)
                at = row + 32 * q
                left_part[at : at + 32, cols] = upper
                left_part[at + 128 : at + 160, cols] = (product - upper.astype(F32)).astype(jnp.bfloat16)

        def direct(k, carry):
            at = (w, k // 2, k % 2)
            cols = pl.ds(pl.multiple_of(k * CAP, CAP), CAP)
            samples = got_r[at]
            products(got_w[at], 0, samples, cols)
            spot = samples[:, 1024:1280].astype(jnp.int32)
            for i in range(8):
                row = lax.broadcasted_iota(jnp.int32, (128, CAP), 0) + 128 * i
                onehot[128 * i : 128 * i + 128, cols] = jnp.where(row == spot, 1.0, 0.0).astype(jnp.bfloat16)
            return carry

        lax.fori_loop(0, 8, direct, 0)

        def shared(k, carry):
            at = (w, k // 2, k % 2)
            cols = pl.ds(pl.multiple_of(k * CAP, CAP), CAP)
            nodes = jnp.concatenate([right[at], left[at]], axis=0)
            products(nodes, 256, got_r[at], cols)
            return carry

        def columns(first, count):
            def body(j, carry):
                at = pl.ds(pl.multiple_of(j * 256, 256), 256)
                part = slice(first, first + count)
                total[j, part] = total[j, part] + lax.dot_general(
                    left_part[part, :], onehot[at, :], (((1,), (1,)), ((), ())), preferred_element_type=F32
                )
                return carry

            lax.fori_loop(0, 4, body, 0)

        @pl.when(w < 3)
        def _():
            receive(w + 1)

        @pl.when(w == 0)
        def _():
            start(3)

        @pl.when(w == 3)
        def _():
            columns(0, 256)

        for copy in shares(w):
            copy.wait_recv()
        lax.fori_loop(0, 8, shared, 0)

        @pl.when(w < 3)
        def _():
            columns(0, 512)

        @pl.when(w == 3)
        def _():
            columns(256, 256)

        between(w)
        return carry

    total[...] = jnp.zeros_like(total)
    lax.fori_loop(0, 4, add, 0)


def spread_sources(total, src):
    x = lax.axis_index("event") // 2

    def tile(i, carry):
        q, r = i // 8, i % 8
        goal = q * 8 + (r // 2 + x) % 4 * 2 + r % 2
        row = r // 4 * 256 + q * 32 + r % 4 * 8
        upper, lower = pl.ds(pl.multiple_of(row, 8), 8), pl.ds(pl.multiple_of(row + 128, 8), 8)
        sums = [total[j, upper, :] + total[j, lower, :] for j in range(4)]
        for j in range(8):
            src[pl.ds(pl.multiple_of(goal * 64 + j * 8, 8), 8), :] = sums[j // 2][:, j % 2 * 128 : j % 2 * 128 + 128]
        return carry

    lax.fori_loop(0, 32, tile, 0)


def row_of(n):
    return n // 8 * 64 + n % 8


def strided(base):
    return pl.ds(base, 8, stride=8)


def tile_of(n):
    return pl.ds(pl.multiple_of(n * 8, 8), 8)


def element_masks():
    sub = lax.broadcasted_iota(jnp.int32, (8, 128), 0)
    lane = lax.broadcasted_iota(jnp.int32, (8, 128), 1)
    return sub, lane


def from_before_x(v):
    sub, lane = element_masks()
    return jnp.where((lane & 15) != 0, pltpu.roll(v, 1, 1), 0.0)


def from_before_y(v):
    sub, lane = element_masks()
    turned = pltpu.roll(v, 16, 1)
    moved = jnp.where(lane < 16, pltpu.roll(turned, 1, 0), turned)
    return jnp.where(((sub & 1) != 0) | (lane >= 16), moved, 0.0)


def after_x(v, old):
    sub, lane = element_masks()
    return jnp.where((lane & 15) != 15, pltpu.roll(v, 127, 1), old)


def after_y(v, old):
    sub, lane = element_masks()
    turned = pltpu.roll(v, 112, 1)
    moved = jnp.where(lane >= 112, pltpu.roll(turned, 7, 0), turned)
    return jnp.where(((sub & 1) != 1) | (lane < 112), moved, old)


def stiffness(now, local, stiff, terms, first, fields=(0, 1, 2, 3)):
    def line(nodes, fresh, fresh_terms):
        mu = [stiff[n] for n in nodes]
        sums = [None] * 4
        for e in range(2):
            g = []
            for f in (e, e + 2):
                if f not in fields and 2 not in fields:
                    continue
                grad = gradient([now[f * 64 + n] for n in nodes])
                g.append(grad)
                if f not in fields:
                    continue
                out = divergence([a * b for a, b in zip(grad, mu)])
                for n, value in zip(nodes, out):
                    local[f * 64 + n] = value if fresh else local[f * 64 + n] + value
            if 2 in fields:
                for i in range(4):
                    pair = g[0][i] * g[1][i]
                    sums[i] = pair if e == 0 else sums[i] + pair
        if 2 in fields:
            for n, value in zip(nodes, sums):
                terms[tile_of(n), :] = value if fresh_terms else terms[tile_of(n), :] + value

    def along_a(l, carry):
        line([4 * l + i for i in range(4)], True, first)
        return carry

    def along_b(l, carry):
        line([l // 4 * 16 + l % 4 + 4 * i for i in range(4)], False, False)
        return carry

    def along_c(l, carry):
        line([l + 16 * i for i in range(4)], False, False)
        return carry

    for body in (along_a, along_b, along_c):
        lax.fori_loop(0, 16, body, 0)


def assemble_xy(local, first, count):
    def along(gap, node_of, from_before, after):
        def lines(i, carry):
            at = [first * 64 + i * 64 + node_of(k) for k in range(16)]
            low, high = [local[n] for n in at], [local[n + gap] for n in at]
            new = [a + from_before(b) for a, b in zip(low, high)]
            end = [after(a, b) for a, b in zip(new, high)]
            for n, a, b in zip(at, new, end):
                local[n] = a
                local[n + gap] = b
            return carry

        lax.fori_loop(0, count, lines, 0)

    along(3, lambda l: 4 * l, from_before_x, after_x)
    along(12, lambda l: l // 4 * 16 + l % 4, from_before_y, after_y)


def pack_faces(local, faces, first, count):
    sub, lane = element_masks()

    def group(i, carry):
        base = i // 4 * 64 + i % 4 * 4
        low = local[base]
        high = pltpu.roll(local[base + 48], 2, 0)
        for q in range(1, 4):
            low = jnp.where((sub >> 1) == q, pltpu.roll(local[base + q], 2 * q, 0), low)
            high = jnp.where((sub >> 1) == q, pltpu.roll(local[base + 48 + q], (2 * q + 2) % 8, 0), high)
        faces[0, i] = low
        faces[1, i] = high
        return carry

    lax.fori_loop(first * 4, first * 4 + count * 4, group, 0)


def assemble_z(local, got, first, count):
    me = lax.axis_index("space")
    sub, lane = element_masks()

    def group(i, carry):
        base = i // 4 * 64 + i % 4 * 4
        before = jnp.where(me > 0, got[0, i], 0.0)
        after = jnp.where(me < SLABS - 1, got[1, i], 0.0)
        for q in range(4):
            low, high = local[base + q], local[base + 48 + q]
            mine = pltpu.roll(before, (8 - 2 * q) % 8, 0) if q else before
            new = low + jnp.where(sub < 2, mine, pltpu.roll(high, 2, 0))
            theirs = pltpu.roll(after, (6 - 2 * q) % 8, 0) if q < 3 else after
            local[base + q] = new
            local[base + 48 + q] = jnp.where(sub < 6, pltpu.roll(new, 6, 0), high + theirs)
        return carry

    lax.fori_loop(first * 4, first * 4 + count * 4, group, 0)


def inverse_mass(density, got, table, inv):
    me = lax.axis_index("space")
    sub, lane = element_masks()

    def planes(v):
        out = []
        low = v + from_before_x(v)
        for a in (low, v, after_x(low, v)):
            new = a + from_before_y(a)
            out += [(new, a, after_y(new, a))]
        return out

    here = planes(density)
    before = planes(jnp.where(me > 0, got[0], 0.0))
    after = planes(jnp.where(me < SLABS - 1, got[1], 0.0))
    for a in range(3):
        for b in range(3):
            v = here[a][b]
            low = v + jnp.where(sub < 2, pltpu.roll(before[a][b], 2, 0), pltpu.roll(v, 2, 0))
            high = v + jnp.where(sub < 6, pltpu.roll(v, 6, 0), pltpu.roll(after[a][b], 6, 0))
            for c, value in enumerate((low, v, high)):
                table[9 * c + 3 * b + a] = 1.0 / value

    def node(n, carry):
        def part(i):
            return (i + 1) // 2

        at = part(n // 16) * 9 + part(n // 4 % 4) * 3 + part(n % 4)
        inv[n] = table[at] * (inverse_weight(n) * np.float32(STEP_SQUARE))
        return carry

    lax.fori_loop(0, 64, node, 0)


def step_kernel(
    send_w, send_r, fwd_now_h, fwd_prev_h, adj_now_h, adj_prev_h, shear_h, density,
    fwd_last, fwd_before, adj_last, adj_before, pieces,
    fwd_now, fwd_prev, adj_now, adj_prev, shear,
    got_w, got_r, left, right, left_part, onehot, total, src,
    zero, one, local, stiff, inv, table, terms, faces, got_faces, got_density, out_terms,
    sw, rw, sr, rr, fs, fr, hs, hr, ds, dr, ts, tr, ins,
):
    pairs = (
        (fwd_now_h, fwd_now), (adj_now_h, adj_now), (shear_h, shear), (fwd_prev_h, fwd_prev), (adj_prev_h, adj_prev)
    )
    fetch = [pltpu.make_async_copy(a, b, ins.at[k]) for k, (a, b) in enumerate(pairs)]
    for copy in fetch:
        copy.start()
    me, ev, y, z, c, x, half = coords()
    up, down = (me + 1) % SLABS, (me + SLABS - 1) % SLABS
    barrier = pltpu.get_barrier_semaphore()
    greeted = greet_stations(barrier)
    for k in range(1, EVENT):
        signal(barrier, event=(ev + k) % EVENT)
    signal(barrier, space=up)
    signal(barrier, space=down)

    pl.semaphore_wait(barrier, greeted + EVENT - 1 + 2)

    weigh = [
        copy_to(density, got_density.at[1], ds.at[1], dr.at[1], space=down),
        copy_to(density, got_density.at[0], ds.at[0], dr.at[0], space=up),
    ]
    for copy in weigh:
        copy.start()
    stations = (send_w, send_r, got_w, got_r, sw, rw, sr, rr)

    def start(w):
        for copy in station_copies(w, False, *stations):
            copy.start()

    def receive(w):
        receive_stations(w, got_w, got_r, left, right, rw, rr, fs, fr)

    def shares(w):
        return share_copies(w, got_w, left, right, fs, fr)

    first_wave = station_copies(0, True, *stations)
    for copy in first_wave:
        copy.start()
    own_stations(send_w, send_r, got_w, got_r, rw, rr)
    start(1)

    for copy in fetch:
        copy.wait()

    def load(n, carry):
        for f, ref in enumerate((fwd_now, adj_now)):
            for e in range(2):
                zero[(2 * f + e) * 64 + n] = ref[strided(e * 512 + row_of(n)), :]
        stiff[n] = shear[strided(row_of(n)), :] * node_weight(n)
        return carry

    lax.fori_loop(0, 64, load, 0)

    def exchange(step, first, count):
        assemble_xy(local, first, count)
        pack_faces(local, faces.at[step], first, count)
        at, k = slice(first * 4, first * 4 + count * 4), first // 2
        halo = [
            copy_to(faces.at[step, 0, at], got_faces.at[step, 1, at], hs.at[step, k, 0], hr.at[step, k, 0], space=down),
            copy_to(faces.at[step, 1, at], got_faces.at[step, 0, at], hs.at[step, k, 1], hr.at[step, k, 1], space=up),
        ]
        for copy in halo:
            copy.start()
        return halo

    def advance(step, first, count):
        assemble_z(local, got_faces.at[step], first, count)

        def update(n, carry):
            mine = inv[n]
            for f in range(first, first + count):
                at, row = f * 64 + n, strided(f % 2 * 512 + row_of(n))
                if step == 0:
                    old = (fwd_prev, adj_prev)[f // 2][row, :]
                    new = 2.0 * zero[at] - old - local[at] * mine
                    one[at] = new
                    (fwd_before, adj_before)[f // 2][row, :] = new
                else:
                    (fwd_last, adj_last)[f // 2][row, :] = 2.0 * one[at] - zero[at] - local[at] * mine
            return carry

        lax.fori_loop(0, 64, update, 0)

    def subtract(step):
        def less(n, carry):
            for e in range(2):
                at = (2 + e) * 64 + n
                local[at] = local[at] - src[strided((2 * e + step) * 512 + row_of(n)), :]
            return carry

        lax.fori_loop(0, 64, less, 0)

    stiffness(zero, local, stiff, terms, True)
    receive(0)
    start(2)
    forward = exchange(0, 0, 2)

    def between(w):
        @pl.when(w == 0)
        def _():
            for copy in weigh:
                copy.wait_recv()
            inverse_mass(density[...], got_density, table, inv)

        @pl.when(w == 2)
        def _():
            for copy in forward:
                copy.wait_recv()
            advance(0, 0, 2)
            stiffness(one, local, stiff, terms, False, (0, 1))

    gather_sources(got_w, got_r, left, right, left_part, onehot, total, receive, start, between, shares)
    spread_sources(total, src)
    subtract(0)
    adjoint = exchange(0, 2, 2)
    forward_last = exchange(1, 0, 2)
    for copy in adjoint:
        copy.wait_recv()
    advance(0, 2, 2)

    stiffness(one, local, stiff, terms, False, (2, 3))

    def cut(j, carry):
        out_terms[j] = terms[pl.ds(j, 64, stride=8), :]
        return carry

    lax.fori_loop(0, EVENT, cut, 0)
    given = []
    for k in range(1, EVENT):
        goal = (ev + k) % EVENT
        given.append(copy_to(out_terms.at[goal], pieces.at[k], ts.at[k], tr.at[k], event=goal))
    for copy in given:
        copy.start()
    subtract(1)
    adjoint_last = exchange(1, 2, 2)
    pieces[0] = out_terms[ev]
    for copy in forward_last:
        copy.wait_recv()
    advance(1, 0, 2)
    for copy in adjoint_last:
        copy.wait_recv()
    advance(1, 2, 2)
    for copy in given:
        copy.wait_recv()

    for copy in first_wave + weigh + forward + adjoint + forward_last + adjoint_last + given:
        copy.wait_send()

    def last(w, carry):
        for copy in station_copies(w, False, *stations):
            copy.wait_send()
        return carry

    lax.fori_loop(1, 4, last, 0)

    def last_shares(w, carry):
        for copy in shares(w):
            copy.wait_send()
        return carry

    lax.fori_loop(0, 4, last_shares, 0)


def steps(send_w, send_r, fwd_now, fwd_prev, adj_now, adj_prev, shear, density):
    fields = pltpu.VMEM((256, 8, 128), F32)
    waves = DMA((4, 4, 2))
    return pl.pallas_call(
        step_kernel,
        out_shape=(
            *[jax.ShapeDtypeStruct((1024, 128), F32)] * 4,
            jax.ShapeDtypeStruct((EVENT, 64, 128), F32),
        ),
        in_specs=[VM, VM, HBM, HBM, HBM, HBM, HBM, VM],
        out_specs=(VM,) * 5,
        scratch_shapes=[
            *[pltpu.VMEM((1024, 128), F32)] * 4,
            pltpu.VMEM((512, 128), F32),
            pltpu.VMEM((4, 4, 2, DIRECT, CAP), F32),
            pltpu.VMEM((4, 4, 2, 1, 5 * CAP), F32),
            pltpu.VMEM((4, 4, 2, 16, CAP), F32),
            pltpu.VMEM((4, 4, 2, 16, CAP), F32),
            pltpu.VMEM((512, 8 * CAP), jnp.bfloat16),
            pltpu.VMEM((ELEMS, 8 * CAP), jnp.bfloat16),
            pltpu.VMEM((4, 512, 256), F32),
            pltpu.VMEM((2048, 128), F32),
            fields,
            fields,
            fields,
            pltpu.VMEM((64, 8, 128), F32),
            pltpu.VMEM((64, 8, 128), F32),
            pltpu.VMEM((27, 8, 128), F32),
            pltpu.VMEM((512, 128), F32),
            pltpu.VMEM((2, 2, 16, 8, 128), F32),
            pltpu.VMEM((2, 2, 16, 8, 128), F32),
            pltpu.VMEM((2, 8, 128), F32),
            pltpu.VMEM((EVENT, 64, 128), F32),
            waves, waves, waves, waves,
            DMA((4, 2)), DMA((4, 2)),
            DMA((2, 2, 2)), DMA((2, 2, 2)),
            DMA((2,)), DMA((2,)),
            DMA((EVENT,)), DMA((EVENT,)),
            DMA((5,)),
        ],
        compiler_params=pltpu.CompilerParams(collective_id=0, has_side_effects=True, vmem_limit_bytes=32 << 20),
        name="steps",
    )(send_w, send_r, fwd_now, fwd_prev, adj_now, adj_prev, shear, density)


def finish_kernel(a, b, c, d, pieces, shear, a_out, b_out, c_out, d_out, kernel_out, kernel, sems):
    ev = lax.axis_index("event")
    copies = [
        pltpu.make_async_copy(src, dst, sems.at[k])
        for k, (src, dst) in enumerate(((a, a_out), (b, b_out), (c, c_out), (d, d_out), (kernel, kernel_out)))
    ]
    for copy in copies[:4]:
        copy.start()
    for i in range(8):
        rows = slice(8 * i, 8 * i + 8)
        total = pieces[0, rows]
        for k in range(1, EVENT):
            total = total + pieces[k, rows]
        n = 8 * i + lax.broadcasted_iota(jnp.int32, (8, 128), 0)
        edge = [((n >> 2 * k) & 3) * (3 - ((n >> 2 * k) & 3)) == 0 for k in range(3)]
        weight = [jnp.where(e, np.float32(1.0 / 6.0), np.float32(5.0 / 6.0)) for e in edge]
        factor = weight[0] * weight[1] * weight[2] * np.float32(-TIME_STEP)
        kernel[rows, :] = total * (factor * shear[pl.ds(pl.multiple_of(i * 64 + ev * 8, 8), 8), :])
    copies[4].start()
    for copy in copies:
        copy.wait()


def finish(*given):
    return pl.pallas_call(
        finish_kernel,
        out_shape=(*[jax.ShapeDtypeStruct((1024, 128), F32)] * 4, jax.ShapeDtypeStruct((64, 128), F32)),
        in_specs=[VM] * 6,
        out_specs=(HBM,) * 5,
        scratch_shapes=[pltpu.VMEM((64, 128), F32), DMA((5,))],
        compiler_params=pltpu.CompilerParams(vmem_limit_bytes=8 << 20),
        name="finish",
    )(*given)


def to_rows(field):
    count = field.size // (64 * ELEMS)
    return field.reshape(count, 8, 8, 8, 128).transpose(0, 1, 3, 2, 4).reshape(count * 512, 128)


def from_rows(rows):
    return rows.reshape(2, 8, 8, 8, 128).transpose(0, 1, 3, 2, 4).reshape(2, 64, ELEMS)


def shards(
    fwd_now, fwd_prev, adj_now, adj_prev, shear_mod, density, station_owner, receiver_local, station_weights, adj_records
):
    def far(value):
        return pltpu.with_memory_space_constraint(value, pltpu.HBM)

    shear = to_rows(shear_mod)
    send_w, send_r = place(
        far(station_owner.T), far(receiver_local.reshape(1, ST)), far(station_weights), far(adj_records)
    )
    found = steps(
        send_w, send_r, *[far(to_rows(v)) for v in (fwd_now, fwd_prev, adj_now, adj_prev)],
        shear, density.reshape(8, 128),
    )
    *fields, kernel = finish(*found, shear)
    return (*map(from_rows, fields), kernel)


def solution(mesh):
    fields = P("event", None, "space")
    return jax.shard_map(
        shards,
        mesh=mesh,
        in_specs=(
            fields, fields, fields, fields,
            P(None, "space"), P("space"), P("space", None), P("space"), P(None, "space"), fields,
        ),
        out_specs=(fields, fields, fields, fields, P(None, ("space", "event"))),
        check_vma=False,
    )
```

```python
import jax
import jax.numpy as jnp
import numpy as np
from jax import lax
from jax.experimental import pallas as pl
from jax.experimental.pallas import tpu as pltpu
from jax.sharding import PartitionSpec as P

MESH = pl.DeviceIdType.MESH
DMA = pltpu.SemaphoreType.DMA
VM = pl.BlockSpec(memory_space=pltpu.VMEM)
HBM = pl.BlockSpec(memory_space=pltpu.HBM)
F32 = jnp.float32
SLABS, EVENT, CAP, ST, ELEMS = 32, 8, 256, 2048, 1024
DIRECT = 32
TIME_STEP, STEP_SQUARE = 0.08, 0.0064


def derivative_table():
    root = 1.0 / np.sqrt(5.0)
    p = np.array([-1.0, -root, root, 1.0])
    d = np.zeros((4, 4))
    for i in range(4):
        for j in range(4):
            if i == j:
                d[i, i] = sum(1.0 / (p[i] - p[k]) for k in range(4) if k != i)
            else:
                upper = np.prod([p[i] - p[k] for k in range(4) if k not in (i, j)])
                lower = np.prod([p[j] - p[k] for k in range(4) if k != j])
                d[i, j] = upper / lower
    return d


D = derivative_table()
ALPHA, BETA = float((D[0, 0] + D[0, 3]) / 2), float((D[1, 0] + D[1, 3]) / 2)
B00, B01 = float((D[0, 0] - D[0, 3]) / 2), float((D[0, 1] - D[0, 2]) / 2)
B10, B11 = float((D[1, 0] - D[1, 3]) / 2), float((D[1, 1] - D[1, 2]) / 2)


def gradient(f):
    e, o0, o1 = (f[0] + f[3]) - (f[1] + f[2]), f[0] - f[3], f[1] - f[2]
    a0, a1 = ALPHA * e, BETA * e
    b0, b1 = B00 * o0 + B01 * o1, B10 * o0 + B11 * o1
    return [b0 + a0, b1 + a1, b1 - a1, b0 - a0]


def divergence(t):
    e0, e1, o0, o1 = t[0] + t[3], t[1] + t[2], t[0] - t[3], t[1] - t[2]
    r = ALPHA * o0 + BETA * o1
    q0, q1 = B00 * e0 + B10 * e1, B01 * e0 + B11 * e1
    return [r + q0, q1 - r, -q1 - r, r - q0]


def point_weight(i):
    return jnp.where((i == 0) | (i == 3), np.float32(1.0 / 6.0), np.float32(5.0 / 6.0))


def coords():
    me, ev = lax.axis_index("space"), lax.axis_index("event")
    return me, ev, me // 8, me // 2 % 4, me % 2, ev // 2, ev % 2


def copy_to(src, dst, send, recv, **where):
    return pltpu.make_async_remote_copy(
        src_ref=src, dst_ref=dst, send_sem=send, recv_sem=recv, device_id=where, device_id_type=MESH
    )


def signal(barrier, inc=1, **where):
    pl.semaphore_signal(barrier, inc=inc, device_id=where, device_id_type=MESH)


def place_kernel(
    owner_h, ids_h, weights_h, records_h, send_w, send_r,
    owner, ids, weights, records, tail, rows, placed, spots_v, spots, sem, ins,
):
    x = lax.axis_index("event") // 2
    fetch = [
        pltpu.make_async_copy(a, b, ins.at[k])
        for k, (a, b) in enumerate(((owner_h, owner), (ids_h, ids), (records_h, records), (weights_h, weights)))
    ]
    for copy in fetch:
        copy.start()
    fetch[0].wait()
    slab = lax.broadcasted_iota(jnp.int32, (SLABS, 256), 0)
    earlier = (
        lax.broadcasted_iota(jnp.int32, (256, 256), 0) < lax.broadcasted_iota(jnp.int32, (256, 256), 1)
    ).astype(F32).astype(jnp.bfloat16)
    named = [jnp.where(owner[:, 256 * b : 256 * b + 256] == slab, 1.0, 0.0).astype(F32) for b in range(8)]
    counts = jnp.dot(
        jnp.concatenate(named, axis=0).astype(jnp.bfloat16), earlier, preferred_element_type=F32
    )
    carry, found = jnp.zeros((SLABS, 1), F32), []
    for b in range(8):
        rank = jnp.sum(named[b] * (counts[32 * b : 32 * b + 32] + carry), axis=0, keepdims=True)
        carry = carry + jnp.sum(named[b], axis=1, keepdims=True)
        found.append(owner[:, 256 * b : 256 * b + 256] * CAP + rank.astype(jnp.int32))
    for b in range(4):
        spots_v[b : b + 1, :] = found[b] + found[b + 4] * 65536
    copy = pltpu.make_async_copy(spots_v, spots, sem)
    copy.start()
    for k in range(1, 4):
        fetch[k].wait()
    tail[...] = jnp.zeros_like(tail)
    for k in range(4):
        tail[k : k + 1, :] = records[k // 2, k % 2 : k % 2 + 1, :]
    tail[4:5, :] = ids[...].astype(F32)
    for c in range(ST // 128):
        cols = slice(128 * c, 128 * c + 128)
        block = jnp.concatenate(
            [weights[pl.ds(pl.multiple_of((x + q) % 4 * 16, 16), 16), cols] for q in range(DIRECT // 16)]
            + [tail[:, cols], jnp.zeros((120 - DIRECT, 128), F32)],
            axis=0,
        )
        rows[cols, :] = block.T

    def clear(i, carry):
        placed[pl.ds(pl.multiple_of(i * 128, 128), 128), :] = jnp.zeros((128, 128), F32)
        return carry

    lax.fori_loop(0, SLABS * CAP // 128, clear, 0)
    copy.wait()

    def move(i, carry):
        for j in range(16):
            pair = spots[i // 16, i % 16 * 16 + j]
            placed[pl.ds(pair & 65535, 1), :] = rows[pl.ds(i * 16 + j, 1), :]
            placed[pl.ds(pair >> 16, 1), :] = rows[pl.ds(ST // 2 + i * 16 + j, 1), :]
        return carry

    lax.fori_loop(0, ST // 32, move, 0)

    def turn(t, carry):
        for h in range(2):
            block = placed[pl.ds(pl.multiple_of(t * CAP + h * 128, 128), 128), :].T
            send_w[t, :, 128 * h : 128 * h + 128] = block[:DIRECT]
            for r in range(5):
                send_r[t, :, 256 * r + 128 * h : 256 * r + 128 * h + 128] = block[DIRECT + r : DIRECT + r + 1]
        return carry

    lax.fori_loop(0, SLABS, turn, 0)


def place(owner, ids, weights, records):
    return pl.pallas_call(
        place_kernel,
        out_shape=(
            jax.ShapeDtypeStruct((SLABS, DIRECT, CAP), F32),
            jax.ShapeDtypeStruct((SLABS, 1, 5 * CAP), F32),
        ),
        in_specs=[HBM] * 4,
        out_specs=(VM, VM),
        scratch_shapes=[
            pltpu.VMEM((1, ST), jnp.int32),
            pltpu.VMEM((1, ST), jnp.int32),
            pltpu.VMEM((64, ST), F32),
            pltpu.VMEM((2, 2, ST), F32),
            pltpu.VMEM((8, ST), F32),
            pltpu.VMEM((ST, 128), F32),
            pltpu.VMEM((SLABS * CAP, 128), F32),
            pltpu.VMEM((4, 256), jnp.int32),
            pltpu.SMEM((4, 256), jnp.int32),
            DMA,
            DMA((4,)),
        ],
        compiler_params=pltpu.CompilerParams(vmem_limit_bytes=12 << 20),
        name="place",
    )(owner, ids, weights, records)


def weight_goal(dy, dz):
    me, ev, y, z, c, x, half = coords()
    deep = half * 4 + z
    step = (0, 1, 7)[dz] if dz < 3 else 2 + 4 * ((deep // 2 + dy) % 2)
    deep = (deep + step) % 8
    return (y + dy) % 4 * 8 + deep % 4 * 2, x * 2 + deep // 4


def record_goal(dy, dz):
    me, ev, y, z, c, x, half = coords()
    return (y + dy) % 4 * 8 + (z + (0, 1, 3, 2)[dz]) % 4 * 2


def greet_stations(barrier):
    me, ev, y, z, c, x, half = coords()
    for dy in range(4):
        for dz in range(4):
            if dy == 0 and dz == 0:
                signal(barrier, 2, space=me + 1 - 2 * c)
                continue
            goal, event = weight_goal(dy, dz)
            other = record_goal(dy, dz)
            for c2 in range(2):
                signal(barrier, space=goal + c2, event=event)
                signal(barrier, space=other + c2)
    signal(barrier, event=(ev + 2) % 8)
    signal(barrier, event=(ev + 6) % 8)
    return 64


def own_stations(send_w, send_r, got_w, got_r, rw, rr):
    me, ev, y, z, c, x, half = coords()
    here = (0, 0, c)
    pltpu.make_async_copy(send_w.at[me], got_w.at[here], rw.at[here]).start()
    pltpu.make_async_copy(send_r.at[me], got_r.at[here], rr.at[here]).start()


def station_copies(dy, first, send_w, send_r, got_w, got_r, sw, rw, sr, rr):
    me, ev, y, z, c, x, half = coords()
    copies = []
    for dz in range(4):
        for c2 in range(2):
            if first and dz == 0:
                if c2 == 0:
                    continue
                goal = other = me + 1 - 2 * c
                event = ev
            else:
                goal, event = weight_goal(dy, dz)
                goal, other = goal + c2, record_goal(dy, dz) + c2
            mine, there = (dy, dz, c2), (dy, dz, c)
            copies += [
                copy_to(send_w.at[goal], got_w.at[there], sw.at[mine], rw.at[there], space=goal, event=event),
                copy_to(send_r.at[other], got_r.at[there], sr.at[mine], rr.at[there], space=other),
            ]
    return copies


def share_copies(w, got_w, left, right, fs, fr):
    ev = lax.axis_index("event")
    return (
        copy_to(got_w.at[w, :, :, 0:16], left.at[w], fs.at[w, 0], fr.at[w, 0], event=(ev + 2) % 8),
        copy_to(got_w.at[w, :, :, 16:32], right.at[w], fs.at[w, 1], fr.at[w, 1], event=(ev + 6) % 8),
    )


def receive_stations(w, got_w, got_r, left, right, rw, rr, fs, fr):
    for dz in range(4):
        for cs in range(2):
            at = (w, dz, cs)
            pltpu.make_async_copy(got_w.at[at], got_w.at[at], rw.at[at]).wait()
            pltpu.make_async_copy(got_r.at[at], got_r.at[at], rr.at[at]).wait()
    for copy in share_copies(w, got_w, left, right, fs, fr):
        copy.start()


def gather_sources(got_w, got_r, left, right, left_part, onehot, total, receive, start, shares):
    def add(w, carry):
        def products(nodes, row, samples, cols):
            for q in range(4):
                product = nodes * samples[:, 256 * q : 256 * q + 256]
                upper = product.astype(jnp.bfloat16)
                at = row + 32 * q
                left_part[at : at + 32, cols] = upper
                left_part[at + 128 : at + 160, cols] = (product - upper.astype(F32)).astype(jnp.bfloat16)

        def direct(k, carry):
            at = (w, k // 2, k % 2)
            cols = pl.ds(pl.multiple_of(k * CAP, CAP), CAP)
            samples = got_r[at]
            products(got_w[at], 0, samples, cols)
            spot = samples[:, 1024:1280].astype(jnp.int32)
            for i in range(8):
                row = lax.broadcasted_iota(jnp.int32, (128, CAP), 0) + 128 * i
                onehot[128 * i : 128 * i + 128, cols] = jnp.where(row == spot, 1.0, 0.0).astype(jnp.bfloat16)
            return carry

        lax.fori_loop(0, 8, direct, 0)

        def shared(k, carry):
            at = (w, k // 2, k % 2)
            cols = pl.ds(pl.multiple_of(k * CAP, CAP), CAP)
            nodes = jnp.concatenate([right[at], left[at]], axis=0)
            products(nodes, 256, got_r[at], cols)
            return carry

        def columns(first, count):
            def body(j, carry):
                at = pl.ds(pl.multiple_of(j * 256, 256), 256)
                part = slice(first, first + count)
                total[j, part] = total[j, part] + lax.dot_general(
                    left_part[part, :], onehot[at, :], (((1,), (1,)), ((), ())), preferred_element_type=F32
                )
                return carry

            lax.fori_loop(0, 4, body, 0)

        @pl.when(w < 3)
        def _():
            receive(w + 1)

        @pl.when(w == 0)
        def _():
            start(3)

        @pl.when(w == 3)
        def _():
            columns(0, 256)

        for copy in shares(w):
            copy.wait_recv()
        lax.fori_loop(0, 8, shared, 0)

        @pl.when(w < 3)
        def _():
            columns(0, 512)

        @pl.when(w == 3)
        def _():
            columns(256, 256)

        return carry

    total[...] = jnp.zeros_like(total)
    lax.fori_loop(0, 4, add, 0)


def spread_sources(total, src):
    x = lax.axis_index("event") // 2

    def tile(i, carry):
        q, r = i // 8, i % 8
        goal = q * 8 + (r // 2 + x) % 4 * 2 + r % 2
        row = r // 4 * 256 + q * 32 + r % 4 * 8
        upper, lower = pl.ds(pl.multiple_of(row, 8), 8), pl.ds(pl.multiple_of(row + 128, 8), 8)
        sums = [total[j, upper, :] + total[j, lower, :] for j in range(4)]
        for j in range(8):
            src[pl.ds(pl.multiple_of(goal * 64 + j * 8, 8), 8), :] = sums[j // 2][:, j % 2 * 128 : j % 2 * 128 + 128]
        return carry

    lax.fori_loop(0, 32, tile, 0)


def row_of(n):
    return n // 8 * 64 + n % 8


def strided(base):
    return pl.ds(base, 8, stride=8)


def tile_of(n):
    return pl.ds(pl.multiple_of(n * 8, 8), 8)


def each_node(body):
    def group(g, carry):
        for r in range(8):
            body(g * 8 + r, g * 64 + r)
        return carry

    lax.fori_loop(0, 8, group, 0)


def element_masks():
    sub = lax.broadcasted_iota(jnp.int32, (8, 128), 0)
    lane = lax.broadcasted_iota(jnp.int32, (8, 128), 1)
    return sub, lane


def from_before_x(v):
    sub, lane = element_masks()
    return jnp.where((lane & 15) != 0, pltpu.roll(v, 1, 1), 0.0)


def from_before_y(v):
    sub, lane = element_masks()
    turned = pltpu.roll(v, 16, 1)
    moved = jnp.where(lane < 16, pltpu.roll(turned, 1, 0), turned)
    return jnp.where(((sub & 1) != 0) | (lane >= 16), moved, 0.0)


def after_x(v, old):
    sub, lane = element_masks()
    return jnp.where((lane & 15) != 15, pltpu.roll(v, 127, 1), old)


def after_y(v, old):
    sub, lane = element_masks()
    turned = pltpu.roll(v, 112, 1)
    moved = jnp.where(lane >= 112, pltpu.roll(turned, 7, 0), turned)
    return jnp.where(((sub & 1) != 1) | (lane < 112), moved, old)


def stiffness(now, local, stiff, terms, first, fields=(0, 1, 2, 3)):
    def line(nodes, fresh, fresh_terms):
        mu = [stiff[n] for n in nodes]
        sums = [None] * 4
        for e in range(2):
            g = []
            for f in (e, e + 2):
                if f not in fields and 2 not in fields:
                    continue
                grad = gradient([now[f * 64 + n] for n in nodes])
                g.append(grad)
                if f not in fields:
                    continue
                out = divergence([a * b for a, b in zip(grad, mu)])
                for n, value in zip(nodes, out):
                    local[f * 64 + n] = value if fresh else local[f * 64 + n] + value
            if 2 in fields:
                for i in range(4):
                    pair = g[0][i] * g[1][i]
                    sums[i] = pair if e == 0 else sums[i] + pair
        if 2 in fields:
            for n, value in zip(nodes, sums):
                terms[tile_of(n), :] = value if fresh_terms else terms[tile_of(n), :] + value

    def along_a(l, carry):
        line([4 * l + i for i in range(4)], True, first)
        return carry

    def along_b(l, carry):
        line([l // 4 * 16 + l % 4 + 4 * i for i in range(4)], False, False)
        return carry

    def along_c(l, carry):
        line([l + 16 * i for i in range(4)], False, False)
        return carry

    for body in (along_a, along_b, along_c):
        lax.fori_loop(0, 16, body, 0)


def assemble_xy(local, first, count):
    def along(gap, node_of, from_before, after):
        def lines(i, carry):
            at = [first * 64 + i * 64 + node_of(k) for k in range(16)]
            low, high = [local[n] for n in at], [local[n + gap] for n in at]
            new = [a + from_before(b) for a, b in zip(low, high)]
            end = [after(a, b) for a, b in zip(new, high)]
            for n, a, b in zip(at, new, end):
                local[n] = a
                local[n + gap] = b
            return carry

        lax.fori_loop(0, count, lines, 0)

    along(3, lambda l: 4 * l, from_before_x, after_x)
    along(12, lambda l: l // 4 * 16 + l % 4, from_before_y, after_y)


def pack_faces(local, faces, first, count):
    sub, lane = element_masks()

    def group(i, carry):
        base = i // 4 * 64 + i % 4 * 4
        low = local[base]
        high = pltpu.roll(local[base + 48], 2, 0)
        for q in range(1, 4):
            low = jnp.where((sub >> 1) == q, pltpu.roll(local[base + q], 2 * q, 0), low)
            high = jnp.where((sub >> 1) == q, pltpu.roll(local[base + 48 + q], (2 * q + 2) % 8, 0), high)
        faces[0, i] = low
        faces[1, i] = high
        return carry

    lax.fori_loop(first * 4, first * 4 + count * 4, group, 0)


def assemble_z(local, got, first, count):
    me = lax.axis_index("space")
    sub, lane = element_masks()

    def group(i, carry):
        base = i // 4 * 64 + i % 4 * 4
        before = jnp.where(me > 0, got[0, i], 0.0)
        after = jnp.where(me < SLABS - 1, got[1, i], 0.0)
        for q in range(4):
            low, high = local[base + q], local[base + 48 + q]
            mine = pltpu.roll(before, (8 - 2 * q) % 8, 0) if q else before
            new = low + jnp.where(sub < 2, mine, pltpu.roll(high, 2, 0))
            theirs = pltpu.roll(after, (6 - 2 * q) % 8, 0) if q < 3 else after
            local[base + q] = new
            local[base + 48 + q] = jnp.where(sub < 6, pltpu.roll(new, 6, 0), high + theirs)
        return carry

    lax.fori_loop(first * 4, first * 4 + count * 4, group, 0)


def inverse_mass(density, got, inv):
    me = lax.axis_index("space")
    sub, lane = element_masks()

    def planes(v):
        out = []
        low = v + from_before_x(v)
        for a in (low, v, after_x(low, v)):
            new = a + from_before_y(a)
            out += [(new, a, after_y(new, a))]
        return out

    here = planes(density)
    before = planes(jnp.where(me > 0, got[0], 0.0))
    after = planes(jnp.where(me < SLABS - 1, got[1], 0.0))
    for a in range(3):
        for b in range(3):
            v = here[a][b]
            low = v + jnp.where(sub < 2, pltpu.roll(before[a][b], 2, 0), pltpu.roll(v, 2, 0))
            high = v + jnp.where(sub < 6, pltpu.roll(v, 6, 0), pltpu.roll(after[a][b], 6, 0))
            for c, value in enumerate((low, v, high)):
                inverse = 1.0 / value
                for n in range(64):
                    at = n % 4, n // 4 % 4, n // 16
                    if tuple((i + 1) // 2 for i in at) == (a, b, c):
                        weight = np.prod([1.2 if i in (1, 2) else 6.0 for i in at])
                        inv[n] = inverse * np.float32(STEP_SQUARE * weight)


def step_kernel(
    send_w, send_r, fwd_now_h, fwd_prev_h, adj_now_h, adj_prev_h, shear_h, density,
    fwd_last, fwd_before, adj_last, adj_before, pieces,
    fwd_now, fwd_prev, adj_now, adj_prev, shear,
    got_w, got_r, left, right, left_part, onehot, total, src,
    zero, one, local, stiff, inv, terms, faces, got_faces, got_density, out_terms, got_terms,
    sw, rw, sr, rr, fs, fr, hs, hr, ds, dr, ts, tr, ins,
):
    pairs = (
        (fwd_now_h, fwd_now), (adj_now_h, adj_now), (shear_h, shear), (fwd_prev_h, fwd_prev), (adj_prev_h, adj_prev)
    )
    fetch = [pltpu.make_async_copy(a, b, ins.at[k]) for k, (a, b) in enumerate(pairs)]
    for copy in fetch:
        copy.start()
    me, ev, y, z, c, x, half = coords()
    up, down = (me + 1) % SLABS, (me + SLABS - 1) % SLABS
    barrier = pltpu.get_barrier_semaphore()
    greeted = greet_stations(barrier)
    for k in range(1, 4):
        signal(barrier, event=(ev + 2 * k) % EVENT)
    signal(barrier, event=x * 2 + 1 - half)
    signal(barrier, space=up)
    signal(barrier, space=down)

    pl.semaphore_wait(barrier, greeted + 4 + 2)

    weigh = [
        copy_to(density, got_density.at[1], ds.at[1], dr.at[1], space=down),
        copy_to(density, got_density.at[0], ds.at[0], dr.at[0], space=up),
    ]
    for copy in weigh:
        copy.start()
    stations = (send_w, send_r, got_w, got_r, sw, rw, sr, rr)

    def start(w):
        for copy in station_copies(w, False, *stations):
            copy.start()

    def receive(w):
        receive_stations(w, got_w, got_r, left, right, rw, rr, fs, fr)

    def shares(w):
        return share_copies(w, got_w, left, right, fs, fr)

    first_wave = station_copies(0, True, *stations)
    for copy in first_wave:
        copy.start()
    own_stations(send_w, send_r, got_w, got_r, rw, rr)
    start(1)

    for copy in fetch:
        copy.wait()

    def load(g, carry):
        for r in range(8):
            n, row = g * 8 + r, g * 64 + r
            for f, ref in enumerate((fwd_now, adj_now)):
                for e in range(2):
                    zero[(2 * f + e) * 64 + n] = ref[strided(e * 512 + row), :]
            along_a = np.float32((1.0 / 6.0, 5.0 / 6.0, 5.0 / 6.0, 1.0 / 6.0)[r % 4])
            stiff[n] = shear[strided(row), :] * (point_weight((2 * g + r // 4) % 4) * point_weight(g // 2) * along_a)
        return carry

    lax.fori_loop(0, 8, load, 0)

    def exchange(step, first, count):
        assemble_xy(local, first, count)
        pack_faces(local, faces.at[step], first, count)
        at, k = slice(first * 4, first * 4 + count * 4), first // 2
        halo = [
            copy_to(faces.at[step, 0, at], got_faces.at[step, 1, at], hs.at[step, k, 0], hr.at[step, k, 0], space=down),
            copy_to(faces.at[step, 1, at], got_faces.at[step, 0, at], hs.at[step, k, 1], hr.at[step, k, 1], space=up),
        ]
        for copy in halo:
            copy.start()
        return halo

    def advance(step, first, count):
        assemble_z(local, got_faces.at[step], first, count)

        def update(n, row):
            mine = inv[n]
            for f in range(first, first + count):
                at, rows = f * 64 + n, strided(f % 2 * 512 + row)
                if step == 0:
                    old = (fwd_prev, adj_prev)[f // 2][rows, :]
                    new = 2.0 * zero[at] - old - local[at] * mine
                    one[at] = new
                    (fwd_before, adj_before)[f // 2][rows, :] = new
                else:
                    (fwd_last, adj_last)[f // 2][rows, :] = 2.0 * one[at] - zero[at] - local[at] * mine

        each_node(update)

    def subtract(step):
        def less(n, row):
            for e in range(2):
                at = (2 + e) * 64 + n
                local[at] = local[at] - src[strided((2 * e + step) * 512 + row), :]

        each_node(less)

    def arrived(copies):
        for copy in copies:
            copy.wait_recv()

    stiffness(zero, local, stiff, terms, True)
    forward = exchange(0, 0, 2)
    arrived(weigh)
    inverse_mass(density[...], got_density, inv)
    receive(0)
    start(2)
    gather_sources(got_w, got_r, left, right, left_part, onehot, total, receive, start, shares)
    spread_sources(total, src)
    subtract(0)
    adjoint = exchange(0, 2, 2)

    arrived(forward)
    advance(0, 0, 2)
    stiffness(one, local, stiff, terms, False, (0, 1))
    forward_last = exchange(1, 0, 2)

    arrived(adjoint)
    advance(0, 2, 2)
    stiffness(one, local, stiff, terms, False, (2, 3))

    def cut(j, carry):
        out_terms[j] = terms[pl.ds(j, 64, stride=8), :]
        return carry

    lax.fori_loop(0, EVENT, cut, 0)
    given = []
    for k in range(1, 4):
        goal = (x + k) % 4 * 2
        given.append(
            copy_to(out_terms.at[pl.ds(goal, 2)], got_terms.at[k], ts.at[k], tr.at[k], event=goal + half)
        )
        given[-1].start()
    subtract(1)
    adjoint_last = exchange(1, 2, 2)
    arrived(forward_last)
    advance(1, 0, 2)

    arrived(given)
    for h in range(2):
        got_terms[0, h] = out_terms[x * 2 + h] + got_terms[1, h] + got_terms[2, h] + got_terms[3, h]
    other = copy_to(got_terms.at[0, 1 - half], pieces.at[1], ts.at[0], tr.at[0], event=x * 2 + 1 - half)
    other.start()
    pieces[0] = got_terms[0, half]
    arrived(adjoint_last)
    advance(1, 2, 2)
    other.wait_recv()
    given.append(other)

    for copy in first_wave + weigh + forward + adjoint + forward_last + adjoint_last + given:
        copy.wait_send()

    def last(w, carry):
        for copy in station_copies(w, False, *stations):
            copy.wait_send()
        return carry

    lax.fori_loop(1, 4, last, 0)

    def last_shares(w, carry):
        for copy in shares(w):
            copy.wait_send()
        return carry

    lax.fori_loop(0, 4, last_shares, 0)


def steps(send_w, send_r, fwd_now, fwd_prev, adj_now, adj_prev, shear, density):
    fields = pltpu.VMEM((256, 8, 128), F32)
    waves = DMA((4, 4, 2))
    return pl.pallas_call(
        step_kernel,
        out_shape=(
            *[jax.ShapeDtypeStruct((1024, 128), F32)] * 4,
            jax.ShapeDtypeStruct((2, 64, 128), F32),
        ),
        in_specs=[VM, VM, HBM, HBM, HBM, HBM, HBM, VM],
        out_specs=(VM,) * 5,
        scratch_shapes=[
            *[pltpu.VMEM((1024, 128), F32)] * 4,
            pltpu.VMEM((512, 128), F32),
            pltpu.VMEM((4, 4, 2, DIRECT, CAP), F32),
            pltpu.VMEM((4, 4, 2, 1, 5 * CAP), F32),
            pltpu.VMEM((4, 4, 2, 16, CAP), F32),
            pltpu.VMEM((4, 4, 2, 16, CAP), F32),
            pltpu.VMEM((512, 8 * CAP), jnp.bfloat16),
            pltpu.VMEM((ELEMS, 8 * CAP), jnp.bfloat16),
            pltpu.VMEM((4, 512, 256), F32),
            pltpu.VMEM((2048, 128), F32),
            fields,
            fields,
            fields,
            pltpu.VMEM((64, 8, 128), F32),
            pltpu.VMEM((64, 8, 128), F32),
            pltpu.VMEM((512, 128), F32),
            pltpu.VMEM((2, 2, 16, 8, 128), F32),
            pltpu.VMEM((2, 2, 16, 8, 128), F32),
            pltpu.VMEM((2, 8, 128), F32),
            pltpu.VMEM((EVENT, 64, 128), F32),
            pltpu.VMEM((4, 2, 64, 128), F32),
            waves, waves, waves, waves,
            DMA((4, 2)), DMA((4, 2)),
            DMA((2, 2, 2)), DMA((2, 2, 2)),
            DMA((2,)), DMA((2,)),
            DMA((4,)), DMA((4,)),
            DMA((5,)),
        ],
        compiler_params=pltpu.CompilerParams(collective_id=0, has_side_effects=True, vmem_limit_bytes=32 << 20),
        name="steps",
    )(send_w, send_r, fwd_now, fwd_prev, adj_now, adj_prev, shear, density)


def finish_kernel(a, b, c, d, pieces, shear, a_out, b_out, c_out, d_out, kernel_out, kernel, sems):
    ev = lax.axis_index("event")
    copies = [
        pltpu.make_async_copy(src, dst, sems.at[k])
        for k, (src, dst) in enumerate(((a, a_out), (b, b_out), (c, c_out), (d, d_out), (kernel, kernel_out)))
    ]
    for copy in copies[:4]:
        copy.start()
    for i in range(8):
        rows = slice(8 * i, 8 * i + 8)
        total = pieces[0, rows] + pieces[1, rows]
        n = 8 * i + lax.broadcasted_iota(jnp.int32, (8, 128), 0)
        edge = [((n >> 2 * k) & 3) * (3 - ((n >> 2 * k) & 3)) == 0 for k in range(3)]
        weight = [jnp.where(e, np.float32(1.0 / 6.0), np.float32(5.0 / 6.0)) for e in edge]
        factor = weight[0] * weight[1] * weight[2] * np.float32(-TIME_STEP)
        kernel[rows, :] = total * (factor * shear[pl.ds(pl.multiple_of(i * 64 + ev * 8, 8), 8), :])
    copies[4].start()
    for copy in copies:
        copy.wait()


def finish(*given):
    return pl.pallas_call(
        finish_kernel,
        out_shape=(*[jax.ShapeDtypeStruct((1024, 128), F32)] * 4, jax.ShapeDtypeStruct((64, 128), F32)),
        in_specs=[VM] * 6,
        out_specs=(HBM,) * 5,
        scratch_shapes=[pltpu.VMEM((64, 128), F32), DMA((5,))],
        compiler_params=pltpu.CompilerParams(vmem_limit_bytes=8 << 20),
        name="finish",
    )(*given)


def to_rows(field):
    count = field.size // (64 * ELEMS)
    return field.reshape(count, 8, 8, 8, 128).transpose(0, 1, 3, 2, 4).reshape(count * 512, 128)


def from_rows(rows):
    return rows.reshape(2, 8, 8, 8, 128).transpose(0, 1, 3, 2, 4).reshape(2, 64, ELEMS)


def shards(
    fwd_now, fwd_prev, adj_now, adj_prev, shear_mod, density, station_owner, receiver_local, station_weights, adj_records
):
    def far(value):
        return pltpu.with_memory_space_constraint(value, pltpu.HBM)

    shear = to_rows(shear_mod)
    send_w, send_r = place(
        far(station_owner.T), far(receiver_local.reshape(1, ST)), far(station_weights), far(adj_records)
    )
    found = steps(
        send_w, send_r, *[far(to_rows(v)) for v in (fwd_now, fwd_prev, adj_now, adj_prev)],
        shear, density.reshape(8, 128),
    )
    *fields, kernel = finish(*found, shear)
    return (*map(from_rows, fields), kernel)


def solution(mesh):
    fields = P("event", None, "space")
    return jax.shard_map(
        shards,
        mesh=mesh,
        in_specs=(
            fields, fields, fields, fields,
            P(None, "space"), P("space"), P("space", None), P("space"), P(None, "space"), fields,
        ),
        out_specs=(fields, fields, fields, fields, P(None, ("space", "event"))),
        check_vma=False,
    )
```

```python
import jax
import jax.numpy as jnp
import numpy as np
from jax import lax
from jax.experimental import pallas as pl
from jax.experimental.pallas import tpu as pltpu
from jax.sharding import PartitionSpec as P

MESH = pl.DeviceIdType.MESH
DMA = pltpu.SemaphoreType.DMA
VM = pl.BlockSpec(memory_space=pltpu.VMEM)
HBM = pl.BlockSpec(memory_space=pltpu.HBM)
F32 = jnp.float32
SLABS, EVENT, CAP, ST, ELEMS = 32, 8, 256, 2048, 1024
DIRECT = 32
EARLY = 4
TIME_STEP, STEP_SQUARE = 0.08, 0.0064


def derivative_table():
    root = 1.0 / np.sqrt(5.0)
    p = np.array([-1.0, -root, root, 1.0])
    d = np.zeros((4, 4))
    for i in range(4):
        for j in range(4):
            if i == j:
                d[i, i] = sum(1.0 / (p[i] - p[k]) for k in range(4) if k != i)
            else:
                upper = np.prod([p[i] - p[k] for k in range(4) if k not in (i, j)])
                lower = np.prod([p[j] - p[k] for k in range(4) if k != j])
                d[i, j] = upper / lower
    return d


D = derivative_table()
ALPHA, BETA = float((D[0, 0] + D[0, 3]) / 2), float((D[1, 0] + D[1, 3]) / 2)
B00, B01 = float((D[0, 0] - D[0, 3]) / 2), float((D[0, 1] - D[0, 2]) / 2)
B10, B11 = float((D[1, 0] - D[1, 3]) / 2), float((D[1, 1] - D[1, 2]) / 2)


def gradient(f):
    e, o0, o1 = (f[0] + f[3]) - (f[1] + f[2]), f[0] - f[3], f[1] - f[2]
    a0, a1 = ALPHA * e, BETA * e
    b0, b1 = B00 * o0 + B01 * o1, B10 * o0 + B11 * o1
    return [b0 + a0, b1 + a1, b1 - a1, b0 - a0]


def divergence(t):
    e0, e1, o0, o1 = t[0] + t[3], t[1] + t[2], t[0] - t[3], t[1] - t[2]
    r = ALPHA * o0 + BETA * o1
    q0, q1 = B00 * e0 + B10 * e1, B01 * e0 + B11 * e1
    return [r + q0, q1 - r, -q1 - r, r - q0]


def point_weight(i):
    return jnp.where((i == 0) | (i == 3), np.float32(1.0 / 6.0), np.float32(5.0 / 6.0))


def coords():
    me, ev = lax.axis_index("space"), lax.axis_index("event")
    return me, ev, me // 8, me // 2 % 4, me % 2, ev // 2, ev % 2


def copy_to(src, dst, send, recv, **where):
    return pltpu.make_async_remote_copy(
        src_ref=src, dst_ref=dst, send_sem=send, recv_sem=recv, device_id=where, device_id_type=MESH
    )


def signal(barrier, inc=1, **where):
    pl.semaphore_signal(barrier, inc=inc, device_id=where, device_id_type=MESH)


def place_kernel(
    owner_h, ids_h, weights_h, records_h, placed,
    owner, ids, weights, records, tail, rows, spots_v, spots, sem, ins,
):
    x = lax.axis_index("event") // 2
    fetch = [
        pltpu.make_async_copy(a, b, ins.at[k])
        for k, (a, b) in enumerate(((owner_h, owner), (ids_h, ids), (records_h, records), (weights_h, weights)))
    ]
    for copy in fetch:
        copy.start()
    fetch[0].wait()
    slab = lax.broadcasted_iota(jnp.int32, (SLABS, 256), 0)
    earlier = (
        lax.broadcasted_iota(jnp.int32, (256, 256), 0) < lax.broadcasted_iota(jnp.int32, (256, 256), 1)
    ).astype(F32).astype(jnp.bfloat16)
    named = [jnp.where(owner[:, 256 * b : 256 * b + 256] == slab, 1.0, 0.0).astype(F32) for b in range(8)]
    counts = jnp.dot(
        jnp.concatenate(named, axis=0).astype(jnp.bfloat16), earlier, preferred_element_type=F32
    )
    carry, found = jnp.zeros((SLABS, 1), F32), []
    for b in range(8):
        rank = jnp.sum(named[b] * (counts[32 * b : 32 * b + 32] + carry), axis=0, keepdims=True)
        carry = carry + jnp.sum(named[b], axis=1, keepdims=True)
        found.append(owner[:, 256 * b : 256 * b + 256] * CAP + rank.astype(jnp.int32))
    for b in range(4):
        spots_v[b : b + 1, :] = found[b] + found[b + 4] * 65536
    copy = pltpu.make_async_copy(spots_v, spots, sem)
    copy.start()
    for k in range(1, 4):
        fetch[k].wait()
    tail[...] = jnp.zeros_like(tail)
    for k in range(4):
        tail[k : k + 1, :] = records[k // 2, k % 2 : k % 2 + 1, :]
    tail[4:5, :] = ids[...].astype(F32)
    for c in range(ST // 128):
        cols = slice(128 * c, 128 * c + 128)
        block = jnp.concatenate(
            [weights[pl.ds(pl.multiple_of((x + q) % 4 * 16, 16), 16), cols] for q in range(DIRECT // 16)]
            + [tail[:, cols], jnp.zeros((120 - DIRECT, 128), F32)],
            axis=0,
        )
        rows[cols, :] = block.T

    def clear(i, carry):
        placed[pl.ds(pl.multiple_of(i * 128, 128), 128), :] = jnp.zeros((128, 128), F32)
        return carry

    lax.fori_loop(0, SLABS * CAP // 128, clear, 0)
    copy.wait()

    def move(i, carry):
        for j in range(16):
            pair = spots[i // 16, i % 16 * 16 + j]
            placed[pl.ds(pair & 65535, 1), :] = rows[pl.ds(i * 16 + j, 1), :]
            placed[pl.ds(pair >> 16, 1), :] = rows[pl.ds(ST // 2 + i * 16 + j, 1), :]
        return carry

    lax.fori_loop(0, ST // 32, move, 0)


def place(owner, ids, weights, records):
    return pl.pallas_call(
        place_kernel,
        out_shape=jax.ShapeDtypeStruct((SLABS * CAP, 128), F32),
        in_specs=[HBM] * 4,
        out_specs=VM,
        scratch_shapes=[
            pltpu.VMEM((1, ST), jnp.int32),
            pltpu.VMEM((1, ST), jnp.int32),
            pltpu.VMEM((64, ST), F32),
            pltpu.VMEM((2, 2, ST), F32),
            pltpu.VMEM((8, ST), F32),
            pltpu.VMEM((ST, 128), F32),
            pltpu.VMEM((4, 256), jnp.int32),
            pltpu.SMEM((4, 256), jnp.int32),
            DMA,
            DMA((4,)),
        ],
        compiler_params=pltpu.CompilerParams(vmem_limit_bytes=12 << 20),
        name="place",
    )(owner, ids, weights, records)


def wave_shift(w):
    return w + w // 2 - 2 * (w // 3)


def turn_stations(w, placed, send_w, send_r):
    me, ev, y, z, c, x, half = coords()
    base = (y + wave_shift(w)) % 4 * 8

    def block(t, carry):
        slab = base + t
        for h in range(2):
            turned = placed[pl.ds(pl.multiple_of(slab * CAP + h * 128, 128), 128), :].T
            send_w[slab, :, 128 * h : 128 * h + 128] = turned[:DIRECT]
            for r in range(5):
                send_r[slab, :, 256 * r + 128 * h : 256 * r + 128 * h + 128] = turned[DIRECT + r : DIRECT + r + 1]
        return carry

    lax.fori_loop(0, 8, block, 0)


def weight_goal(dy, dz):
    me, ev, y, z, c, x, half = coords()
    deep = half * 4 + z
    step = (0, 1, 7)[dz] if dz < 3 else 2 + 4 * ((deep // 2 + dy) % 2)
    deep = (deep + step) % 8
    return (y + dy) % 4 * 8 + deep % 4 * 2, x * 2 + deep // 4


def record_goal(dy, dz):
    me, ev, y, z, c, x, half = coords()
    return (y + dy) % 4 * 8 + (z + (0, 1, 3, 2)[dz]) % 4 * 2


def greet_stations(barrier):
    me, ev, y, z, c, x, half = coords()
    for dy in range(4):
        for dz in range(4):
            if dy == 0 and dz == 0:
                signal(barrier, 2, space=me + 1 - 2 * c)
                continue
            goal, event = weight_goal(dy, dz)
            other = record_goal(dy, dz)
            for c2 in range(2):
                signal(barrier, space=goal + c2, event=event)
                signal(barrier, space=other + c2)
    signal(barrier, event=(ev + 2) % 8)
    signal(barrier, event=(ev + 6) % 8)
    return 64


def own_stations(send_w, send_r, got_w, got_r, rw, rr):
    me, ev, y, z, c, x, half = coords()
    here = (0, 0, c)
    pltpu.make_async_copy(send_w.at[me], got_w.at[here], rw.at[here]).start()
    pltpu.make_async_copy(send_r.at[me], got_r.at[here], rr.at[here]).start()


def station_copies(w, first, send_w, send_r, got_w, got_r, sw, rw, sr, rr):
    me, ev, y, z, c, x, half = coords()
    copies = []
    for dz in range(4):
        for c2 in range(2):
            if first and dz == 0:
                if c2 == 0:
                    continue
                goal = other = me + 1 - 2 * c
                event = ev
            else:
                goal, event = weight_goal(wave_shift(w), dz)
                goal, other = goal + c2, record_goal(wave_shift(w), dz) + c2
            mine, there = (w, dz, c2), (w, dz, c)
            copies += [
                copy_to(send_w.at[goal], got_w.at[there], sw.at[mine], rw.at[there], space=goal, event=event),
                copy_to(send_r.at[other], got_r.at[there], sr.at[mine], rr.at[there], space=other),
            ]
    return copies


def share_copies(w, got_w, left, right, fs, fr):
    ev = lax.axis_index("event")
    return (
        copy_to(got_w.at[w, :, :, 0:16], left.at[w], fs.at[w, 0], fr.at[w, 0], event=(ev + 2) % 8),
        copy_to(got_w.at[w, :, :, 16:32], right.at[w], fs.at[w, 1], fr.at[w, 1], event=(ev + 6) % 8),
    )


def receive_stations(w, got_w, got_r, left, right, rw, rr, fs, fr):
    for dz in range(4):
        for cs in range(2):
            at = (w, dz, cs)
            pltpu.make_async_copy(got_w.at[at], got_w.at[at], rw.at[at]).wait()
            pltpu.make_async_copy(got_r.at[at], got_r.at[at], rr.at[at]).wait()
    for copy in share_copies(w, got_w, left, right, fs, fr):
        copy.start()


def gather_sources(got_w, got_r, left, right, left_part, onehot, total, receive, start, shares):
    def add(w, carry):
        def products(nodes, row, samples, cols):
            for q in range(4):
                product = nodes * samples[:, 256 * q : 256 * q + 256]
                upper = product.astype(jnp.bfloat16)
                at = row + 32 * q
                left_part[at : at + 32, cols] = upper
                left_part[at + 128 : at + 160, cols] = (product - upper.astype(F32)).astype(jnp.bfloat16)

        def direct(k, carry):
            at = (w, k // 2, k % 2)
            cols = pl.ds(pl.multiple_of(k * CAP, CAP), CAP)
            samples = got_r[at]
            products(got_w[at], 0, samples, cols)
            spot = samples[:, 1024:1280].astype(jnp.int32)
            for i in range(8):
                row = lax.broadcasted_iota(jnp.int32, (128, CAP), 0) + 128 * i
                onehot[128 * i : 128 * i + 128, cols] = jnp.where(row == spot, 1.0, 0.0).astype(jnp.bfloat16)
            return carry

        lax.fori_loop(0, 8, direct, 0)

        def shared(k, carry):
            at = (w, k // 2, k % 2)
            cols = pl.ds(pl.multiple_of(k * CAP, CAP), CAP)
            nodes = jnp.concatenate([right[at], left[at]], axis=0)
            products(nodes, 256, got_r[at], cols)
            return carry

        def columns(first, count):
            def body(j, carry):
                at = pl.ds(pl.multiple_of(j * 256, 256), 256)
                part = slice(first, first + count)
                total[j, part] = total[j, part] + lax.dot_general(
                    left_part[part, :], onehot[at, :], (((1,), (1,)), ((), ())), preferred_element_type=F32
                )
                return carry

            lax.fori_loop(0, 4, body, 0)

        @pl.when(w < 3)
        def _():
            receive(w + 1)

        if EARLY == 2:
            pl.when(w == 0)(lambda: start(3))

        @pl.when(w == 3)
        def _():
            columns(0, 256)

        for copy in shares(w):
            copy.wait_recv()
        lax.fori_loop(0, 8, shared, 0)

        @pl.when(w < 3)
        def _():
            columns(0, 512)

        @pl.when(w == 3)
        def _():
            columns(256, 256)

        return carry

    total[...] = jnp.zeros_like(total)
    lax.fori_loop(0, 4, add, 0)


def spread_sources(total, src):
    x = lax.axis_index("event") // 2

    def tile(i, carry):
        q, r = i // 8, i % 8
        goal = q * 8 + (r // 2 + x) % 4 * 2 + r % 2
        row = r // 4 * 256 + q * 32 + r % 4 * 8
        upper, lower = pl.ds(pl.multiple_of(row, 8), 8), pl.ds(pl.multiple_of(row + 128, 8), 8)
        sums = [total[j, upper, :] + total[j, lower, :] for j in range(4)]
        for j in range(8):
            src[pl.ds(pl.multiple_of(goal * 64 + j * 8, 8), 8), :] = sums[j // 2][:, j % 2 * 128 : j % 2 * 128 + 128]
        return carry

    lax.fori_loop(0, 32, tile, 0)


def row_of(n):
    return n // 8 * 64 + n % 8


def strided(base):
    return pl.ds(base, 8, stride=8)


def tile_of(n):
    return pl.ds(pl.multiple_of(n * 8, 8), 8)


def each_node(body):
    def group(g, carry):
        for r in range(8):
            body(g * 8 + r, g * 64 + r)
        return carry

    lax.fori_loop(0, 8, group, 0)


def element_masks():
    sub = lax.broadcasted_iota(jnp.int32, (8, 128), 0)
    lane = lax.broadcasted_iota(jnp.int32, (8, 128), 1)
    return sub, lane


def from_before_x(v):
    sub, lane = element_masks()
    return jnp.where((lane & 15) != 0, pltpu.roll(v, 1, 1), 0.0)


def from_before_y(v):
    sub, lane = element_masks()
    turned = pltpu.roll(v, 16, 1)
    moved = jnp.where(lane < 16, pltpu.roll(turned, 1, 0), turned)
    return jnp.where(((sub & 1) != 0) | (lane >= 16), moved, 0.0)


def after_x(v, old):
    sub, lane = element_masks()
    return jnp.where((lane & 15) != 15, pltpu.roll(v, 127, 1), old)


def after_y(v, old):
    sub, lane = element_masks()
    turned = pltpu.roll(v, 112, 1)
    moved = jnp.where(lane >= 112, pltpu.roll(turned, 7, 0), turned)
    return jnp.where(((sub & 1) != 1) | (lane < 112), moved, old)


def stiffness(now, local, stiff, terms, first, fields=(0, 1, 2, 3)):
    def line(nodes, fresh, fresh_terms):
        mu = [stiff[n] for n in nodes]
        sums = [None] * 4
        for e in range(2):
            g = []
            for f in (e, e + 2):
                if f not in fields and 2 not in fields:
                    continue
                grad = gradient([now[f * 64 + n] for n in nodes])
                g.append(grad)
                if f not in fields:
                    continue
                out = divergence([a * b for a, b in zip(grad, mu)])
                for n, value in zip(nodes, out):
                    local[f * 64 + n] = value if fresh else local[f * 64 + n] + value
            if 2 in fields:
                for i in range(4):
                    pair = g[0][i] * g[1][i]
                    sums[i] = pair if e == 0 else sums[i] + pair
        if 2 in fields:
            for n, value in zip(nodes, sums):
                terms[tile_of(n), :] = value if fresh_terms else terms[tile_of(n), :] + value

    def along_a(l, carry):
        line([4 * l + i for i in range(4)], True, first)
        return carry

    def along_b(l, carry):
        line([l // 4 * 16 + l % 4 + 4 * i for i in range(4)], False, False)
        return carry

    def along_c(l, carry):
        line([l + 16 * i for i in range(4)], False, False)
        return carry

    for body in (along_a, along_b, along_c):
        lax.fori_loop(0, 16, body, 0)


def assemble_xy(local, first, count):
    def along(gap, node_of, from_before, after):
        def lines(i, carry):
            at = [first * 64 + i * 64 + node_of(k) for k in range(16)]
            low, high = [local[n] for n in at], [local[n + gap] for n in at]
            new = [a + from_before(b) for a, b in zip(low, high)]
            end = [after(a, b) for a, b in zip(new, high)]
            for n, a, b in zip(at, new, end):
                local[n] = a
                local[n + gap] = b
            return carry

        lax.fori_loop(0, count, lines, 0)

    along(3, lambda l: 4 * l, from_before_x, after_x)
    along(12, lambda l: l // 4 * 16 + l % 4, from_before_y, after_y)


def pack_faces(local, faces, first, count):
    sub, lane = element_masks()

    def group(i, carry):
        base = i // 4 * 64 + i % 4 * 4
        low = local[base]
        high = pltpu.roll(local[base + 48], 2, 0)
        for q in range(1, 4):
            low = jnp.where((sub >> 1) == q, pltpu.roll(local[base + q], 2 * q, 0), low)
            high = jnp.where((sub >> 1) == q, pltpu.roll(local[base + 48 + q], (2 * q + 2) % 8, 0), high)
        faces[0, i] = low
        faces[1, i] = high
        return carry

    lax.fori_loop(first * 4, first * 4 + count * 4, group, 0)


def assemble_z(local, got, first, count):
    me = lax.axis_index("space")
    sub, lane = element_masks()

    def group(i, carry):
        base = i // 4 * 64 + i % 4 * 4
        before = jnp.where(me > 0, got[0, i], 0.0)
        after = jnp.where(me < SLABS - 1, got[1, i], 0.0)
        for q in range(4):
            low, high = local[base + q], local[base + 48 + q]
            mine = pltpu.roll(before, (8 - 2 * q) % 8, 0) if q else before
            new = low + jnp.where(sub < 2, mine, pltpu.roll(high, 2, 0))
            theirs = pltpu.roll(after, (6 - 2 * q) % 8, 0) if q < 3 else after
            local[base + q] = new
            local[base + 48 + q] = jnp.where(sub < 6, pltpu.roll(new, 6, 0), high + theirs)
        return carry

    lax.fori_loop(first * 4, first * 4 + count * 4, group, 0)


def inverse_mass(density, got, inv):
    me = lax.axis_index("space")
    sub, lane = element_masks()

    def planes(v):
        out = []
        low = v + from_before_x(v)
        for a in (low, v, after_x(low, v)):
            new = a + from_before_y(a)
            out += [(new, a, after_y(new, a))]
        return out

    here = planes(density)
    before = planes(jnp.where(me > 0, got[0], 0.0))
    after = planes(jnp.where(me < SLABS - 1, got[1], 0.0))
    for a in range(3):
        for b in range(3):
            v = here[a][b]
            low = v + jnp.where(sub < 2, pltpu.roll(before[a][b], 2, 0), pltpu.roll(v, 2, 0))
            high = v + jnp.where(sub < 6, pltpu.roll(v, 6, 0), pltpu.roll(after[a][b], 6, 0))
            for c, value in enumerate((low, v, high)):
                inverse = 1.0 / value
                for n in range(64):
                    at = n % 4, n // 4 % 4, n // 16
                    if tuple((i + 1) // 2 for i in at) == (a, b, c):
                        weight = np.prod([1.2 if i in (1, 2) else 6.0 for i in at])
                        inv[n] = inverse * np.float32(STEP_SQUARE * weight)


def step_kernel(
    placed, fwd_now_h, fwd_prev_h, adj_now_h, adj_prev_h, shear_h, density,
    fwd_last, fwd_before, adj_last, adj_before, pieces,
    fwd_now, fwd_prev, adj_now, adj_prev, shear, send_w, send_r,
    got_w, got_r, left, right, left_part, onehot, total, src,
    zero, one, local, stiff, inv, terms, faces, got_faces, got_density, out_terms, got_terms,
    sw, rw, sr, rr, fs, fr, hs, hr, ds, dr, ts, tr, ins,
):
    pairs = (
        (fwd_now_h, fwd_now), (adj_now_h, adj_now), (shear_h, shear), (fwd_prev_h, fwd_prev), (adj_prev_h, adj_prev)
    )
    fetch = [pltpu.make_async_copy(a, b, ins.at[k]) for k, (a, b) in enumerate(pairs)]
    for copy in fetch:
        copy.start()
    me, ev, y, z, c, x, half = coords()
    up, down = (me + 1) % SLABS, (me + SLABS - 1) % SLABS
    barrier = pltpu.get_barrier_semaphore()
    greeted = greet_stations(barrier)
    for k in range(1, 4):
        signal(barrier, event=(ev + 2 * k) % EVENT)
    signal(barrier, event=x * 2 + 1 - half)
    signal(barrier, space=up)
    signal(barrier, space=down)

    def turn(w):
        turn_stations(w, placed, send_w, send_r)

    turn(0)
    pl.semaphore_wait(barrier, greeted + 4 + 2)

    weigh = [
        copy_to(density, got_density.at[1], ds.at[1], dr.at[1], space=down),
        copy_to(density, got_density.at[0], ds.at[0], dr.at[0], space=up),
    ]
    for copy in weigh:
        copy.start()
    stations = (send_w, send_r, got_w, got_r, sw, rw, sr, rr)

    def start(w):
        for copy in station_copies(w, False, *stations):
            copy.start()

    def receive(w):
        receive_stations(w, got_w, got_r, left, right, rw, rr, fs, fr)

    def shares(w):
        return share_copies(w, got_w, left, right, fs, fr)

    first_wave = station_copies(0, True, *stations)
    for copy in first_wave:
        copy.start()
    own_stations(send_w, send_r, got_w, got_r, rw, rr)
    for w in range(1, EARLY):
        turn(w)
        start(w)

    for copy in fetch:
        copy.wait()

    def load(g, carry):
        for r in range(8):
            n, row = g * 8 + r, g * 64 + r
            for f, ref in enumerate((fwd_now, adj_now)):
                for e in range(2):
                    zero[(2 * f + e) * 64 + n] = ref[strided(e * 512 + row), :]
            along_a = np.float32((1.0 / 6.0, 5.0 / 6.0, 5.0 / 6.0, 1.0 / 6.0)[r % 4])
            stiff[n] = shear[strided(row), :] * (point_weight((2 * g + r // 4) % 4) * point_weight(g // 2) * along_a)
        return carry

    lax.fori_loop(0, 8, load, 0)

    def exchange(step, first, count):
        assemble_xy(local, first, count)
        pack_faces(local, faces.at[step], first, count)
        at, k = slice(first * 4, first * 4 + count * 4), first // 2
        halo = [
            copy_to(faces.at[step, 0, at], got_faces.at[step, 1, at], hs.at[step, k, 0], hr.at[step, k, 0], space=down),
            copy_to(faces.at[step, 1, at], got_faces.at[step, 0, at], hs.at[step, k, 1], hr.at[step, k, 1], space=up),
        ]
        for copy in halo:
            copy.start()
        return halo

    def advance(step, first, count):
        assemble_z(local, got_faces.at[step], first, count)

        def update(n, row):
            mine = inv[n]
            for f in range(first, first + count):
                at, rows = f * 64 + n, strided(f % 2 * 512 + row)
                if step == 0:
                    old = (fwd_prev, adj_prev)[f // 2][rows, :]
                    new = 2.0 * zero[at] - old - local[at] * mine
                    one[at] = new
                    (fwd_before, adj_before)[f // 2][rows, :] = new
                else:
                    (fwd_last, adj_last)[f // 2][rows, :] = 2.0 * one[at] - zero[at] - local[at] * mine

        each_node(update)

    def subtract(step):
        def less(n, row):
            for e in range(2):
                at = (2 + e) * 64 + n
                local[at] = local[at] - src[strided((2 * e + step) * 512 + row), :]

        each_node(less)

    def arrived(copies):
        for copy in copies:
            copy.wait_recv()

    stiffness(zero, local, stiff, terms, True)
    forward = exchange(0, 0, 2)
    arrived(weigh)
    inverse_mass(density[...], got_density, inv)
    for w in range(EARLY, 4):
        turn(w)
    receive(0)
    if EARLY < 4:
        start(EARLY)
    gather_sources(got_w, got_r, left, right, left_part, onehot, total, receive, start, shares)
    spread_sources(total, src)
    subtract(0)
    adjoint = exchange(0, 2, 2)

    arrived(forward)
    advance(0, 0, 2)
    stiffness(one, local, stiff, terms, False, (0, 1))
    forward_last = exchange(1, 0, 2)

    arrived(adjoint)
    advance(0, 2, 2)
    stiffness(one, local, stiff, terms, False, (2, 3))

    def cut(j, carry):
        out_terms[j] = terms[pl.ds(j, 64, stride=8), :]
        return carry

    lax.fori_loop(0, EVENT, cut, 0)
    given = []
    for k in range(1, 4):
        goal = (x + k) % 4 * 2
        given.append(
            copy_to(out_terms.at[pl.ds(goal, 2)], got_terms.at[k], ts.at[k], tr.at[k], event=goal + half)
        )
        given[-1].start()
    subtract(1)
    adjoint_last = exchange(1, 2, 2)
    arrived(forward_last)
    advance(1, 0, 2)

    arrived(given)
    for h in range(2):
        got_terms[0, h] = out_terms[x * 2 + h] + got_terms[1, h] + got_terms[2, h] + got_terms[3, h]
    other = copy_to(got_terms.at[0, 1 - half], pieces.at[1], ts.at[0], tr.at[0], event=x * 2 + 1 - half)
    other.start()
    pieces[0] = got_terms[0, half]
    arrived(adjoint_last)
    advance(1, 2, 2)
    other.wait_recv()
    given.append(other)

    for copy in first_wave + weigh + forward + adjoint + forward_last + adjoint_last + given:
        copy.wait_send()

    def last(w, carry):
        for copy in station_copies(w, False, *stations):
            copy.wait_send()
        return carry

    lax.fori_loop(1, 4, last, 0)

    def last_shares(w, carry):
        for copy in shares(w):
            copy.wait_send()
        return carry

    lax.fori_loop(0, 4, last_shares, 0)


def steps(placed, fwd_now, fwd_prev, adj_now, adj_prev, shear, density):
    fields = pltpu.VMEM((256, 8, 128), F32)
    waves = DMA((4, 4, 2))
    return pl.pallas_call(
        step_kernel,
        out_shape=(
            *[jax.ShapeDtypeStruct((1024, 128), F32)] * 4,
            jax.ShapeDtypeStruct((2, 64, 128), F32),
        ),
        in_specs=[VM, HBM, HBM, HBM, HBM, HBM, VM],
        out_specs=(VM,) * 5,
        scratch_shapes=[
            *[pltpu.VMEM((1024, 128), F32)] * 4,
            pltpu.VMEM((512, 128), F32),
            pltpu.VMEM((SLABS, DIRECT, CAP), F32),
            pltpu.VMEM((SLABS, 1, 5 * CAP), F32),
            pltpu.VMEM((4, 4, 2, DIRECT, CAP), F32),
            pltpu.VMEM((4, 4, 2, 1, 5 * CAP), F32),
            pltpu.VMEM((4, 4, 2, 16, CAP), F32),
            pltpu.VMEM((4, 4, 2, 16, CAP), F32),
            pltpu.VMEM((512, 8 * CAP), jnp.bfloat16),
            pltpu.VMEM((ELEMS, 8 * CAP), jnp.bfloat16),
            pltpu.VMEM((4, 512, 256), F32),
            pltpu.VMEM((2048, 128), F32),
            fields,
            fields,
            fields,
            pltpu.VMEM((64, 8, 128), F32),
            pltpu.VMEM((64, 8, 128), F32),
            pltpu.VMEM((512, 128), F32),
            pltpu.VMEM((2, 2, 16, 8, 128), F32),
            pltpu.VMEM((2, 2, 16, 8, 128), F32),
            pltpu.VMEM((2, 8, 128), F32),
            pltpu.VMEM((EVENT, 64, 128), F32),
            pltpu.VMEM((4, 2, 64, 128), F32),
            waves, waves, waves, waves,
            DMA((4, 2)), DMA((4, 2)),
            DMA((2, 2, 2)), DMA((2, 2, 2)),
            DMA((2,)), DMA((2,)),
            DMA((4,)), DMA((4,)),
            DMA((5,)),
        ],
        compiler_params=pltpu.CompilerParams(collective_id=0, has_side_effects=True, vmem_limit_bytes=32 << 20),
        name="steps",
    )(placed, fwd_now, fwd_prev, adj_now, adj_prev, shear, density)


def finish_kernel(a, b, c, d, pieces, shear, a_out, b_out, c_out, d_out, kernel_out, kernel, sems):
    ev = lax.axis_index("event")
    copies = [
        pltpu.make_async_copy(src, dst, sems.at[k])
        for k, (src, dst) in enumerate(((a, a_out), (b, b_out), (c, c_out), (d, d_out), (kernel, kernel_out)))
    ]
    for copy in copies[:4]:
        copy.start()
    for i in range(8):
        rows = slice(8 * i, 8 * i + 8)
        total = pieces[0, rows] + pieces[1, rows]
        n = 8 * i + lax.broadcasted_iota(jnp.int32, (8, 128), 0)
        edge = [((n >> 2 * k) & 3) * (3 - ((n >> 2 * k) & 3)) == 0 for k in range(3)]
        weight = [jnp.where(e, np.float32(1.0 / 6.0), np.float32(5.0 / 6.0)) for e in edge]
        factor = weight[0] * weight[1] * weight[2] * np.float32(-TIME_STEP)
        kernel[rows, :] = total * (factor * shear[pl.ds(pl.multiple_of(i * 64 + ev * 8, 8), 8), :])
    copies[4].start()
    for copy in copies:
        copy.wait()


def finish(*given):
    return pl.pallas_call(
        finish_kernel,
        out_shape=(*[jax.ShapeDtypeStruct((1024, 128), F32)] * 4, jax.ShapeDtypeStruct((64, 128), F32)),
        in_specs=[VM] * 6,
        out_specs=(HBM,) * 5,
        scratch_shapes=[pltpu.VMEM((64, 128), F32), DMA((5,))],
        compiler_params=pltpu.CompilerParams(vmem_limit_bytes=8 << 20),
        name="finish",
    )(*given)


def to_rows(field):
    count = field.size // (64 * ELEMS)
    return field.reshape(count, 8, 8, 8, 128).transpose(0, 1, 3, 2, 4).reshape(count * 512, 128)


def from_rows(rows):
    return rows.reshape(2, 8, 8, 8, 128).transpose(0, 1, 3, 2, 4).reshape(2, 64, ELEMS)


def shards(
    fwd_now, fwd_prev, adj_now, adj_prev, shear_mod, density, station_owner, receiver_local, station_weights, adj_records
):
    def far(value):
        return pltpu.with_memory_space_constraint(value, pltpu.HBM)

    shear = to_rows(shear_mod)
    placed = place(
        far(station_owner.T), far(receiver_local.reshape(1, ST)), far(station_weights), far(adj_records)
    )
    found = steps(
        placed, *[far(to_rows(v)) for v in (fwd_now, fwd_prev, adj_now, adj_prev)],
        shear, density.reshape(8, 128),
    )
    *fields, kernel = finish(*found, shear)
    return (*map(from_rows, fields), kernel)


def solution(mesh):
    fields = P("event", None, "space")
    return jax.shard_map(
        shards,
        mesh=mesh,
        in_specs=(
            fields, fields, fields, fields,
            P(None, "space"), P("space"), P("space", None), P("space"), P(None, "space"), fields,
        ),
        out_specs=(fields, fields, fields, fields, P(None, ("space", "event"))),
        check_vma=False,
    )
```

```python
import jax
import jax.numpy as jnp
import numpy as np
from jax import lax
from jax.experimental import pallas as pl
from jax.experimental.pallas import tpu as pltpu
from jax.sharding import PartitionSpec as P

MESH = pl.DeviceIdType.MESH
DMA = pltpu.SemaphoreType.DMA
VM = pl.BlockSpec(memory_space=pltpu.VMEM)
HBM = pl.BlockSpec(memory_space=pltpu.HBM)
F32 = jnp.float32
SLABS, EVENT, CAP, ST, ELEMS = 32, 8, 256, 2048, 1024
DIRECT = 32
EARLY = 4
TIME_STEP, STEP_SQUARE = 0.08, 0.0064


def derivative_table():
    root = 1.0 / np.sqrt(5.0)
    p = np.array([-1.0, -root, root, 1.0])
    d = np.zeros((4, 4))
    for i in range(4):
        for j in range(4):
            if i == j:
                d[i, i] = sum(1.0 / (p[i] - p[k]) for k in range(4) if k != i)
            else:
                upper = np.prod([p[i] - p[k] for k in range(4) if k not in (i, j)])
                lower = np.prod([p[j] - p[k] for k in range(4) if k != j])
                d[i, j] = upper / lower
    return d


D = derivative_table()
ALPHA, BETA = float((D[0, 0] + D[0, 3]) / 2), float((D[1, 0] + D[1, 3]) / 2)
B00, B01 = float((D[0, 0] - D[0, 3]) / 2), float((D[0, 1] - D[0, 2]) / 2)
B10, B11 = float((D[1, 0] - D[1, 3]) / 2), float((D[1, 1] - D[1, 2]) / 2)


def gradient(f):
    e, o0, o1 = (f[0] + f[3]) - (f[1] + f[2]), f[0] - f[3], f[1] - f[2]
    a0, a1 = ALPHA * e, BETA * e
    b0, b1 = B00 * o0 + B01 * o1, B10 * o0 + B11 * o1
    return [b0 + a0, b1 + a1, b1 - a1, b0 - a0]


def divergence(t):
    e0, e1, o0, o1 = t[0] + t[3], t[1] + t[2], t[0] - t[3], t[1] - t[2]
    r = ALPHA * o0 + BETA * o1
    q0, q1 = B00 * e0 + B10 * e1, B01 * e0 + B11 * e1
    return [r + q0, q1 - r, -q1 - r, r - q0]


def point_weight(i):
    return jnp.where((i == 0) | (i == 3), np.float32(1.0 / 6.0), np.float32(5.0 / 6.0))


def coords():
    me, ev = lax.axis_index("space"), lax.axis_index("event")
    return me, ev, me // 8, me // 2 % 4, me % 2, ev // 2, ev % 2


def copy_to(src, dst, send, recv, **where):
    return pltpu.make_async_remote_copy(
        src_ref=src, dst_ref=dst, send_sem=send, recv_sem=recv, device_id=where, device_id_type=MESH
    )


def signal(barrier, inc=1, **where):
    pl.semaphore_signal(barrier, inc=inc, device_id=where, device_id_type=MESH)


def place_kernel(
    owner_h, ids_h, weights_h, records_h, placed,
    owner, ids, weights, records, tail, rows, spots_v, spots, sem, ins,
):
    x = lax.axis_index("event") // 2
    fetch = [
        pltpu.make_async_copy(a, b, ins.at[k])
        for k, (a, b) in enumerate(((owner_h, owner), (ids_h, ids), (records_h, records), (weights_h, weights)))
    ]
    for copy in fetch:
        copy.start()

    def clear(i, carry):
        placed[pl.ds(pl.multiple_of(i * 128, 128), 128), :] = jnp.zeros((128, 128), F32)
        return carry

    lax.fori_loop(0, SLABS * CAP // 128, clear, 0)
    fetch[0].wait()
    slab = lax.broadcasted_iota(jnp.int32, (SLABS, 256), 0)
    earlier = (
        lax.broadcasted_iota(jnp.int32, (256, 256), 0) < lax.broadcasted_iota(jnp.int32, (256, 256), 1)
    ).astype(F32).astype(jnp.bfloat16)
    named = [jnp.where(owner[:, 256 * b : 256 * b + 256] == slab, 1.0, 0.0).astype(F32) for b in range(8)]
    counts = jnp.dot(
        jnp.concatenate(named, axis=0).astype(jnp.bfloat16), earlier, preferred_element_type=F32
    )
    carry, found = jnp.zeros((SLABS, 1), F32), []
    for b in range(8):
        rank = jnp.sum(named[b] * (counts[32 * b : 32 * b + 32] + carry), axis=0, keepdims=True)
        carry = carry + jnp.sum(named[b], axis=1, keepdims=True)
        found.append(owner[:, 256 * b : 256 * b + 256] * CAP + rank.astype(jnp.int32))
    for b in range(4):
        spots_v[b : b + 1, :] = found[b] + found[b + 4] * 65536
    copy = pltpu.make_async_copy(spots_v, spots, sem)
    copy.start()
    for k in range(1, 4):
        fetch[k].wait()
    tail[...] = jnp.zeros_like(tail)
    for k in range(4):
        tail[k : k + 1, :] = records[k // 2, k % 2 : k % 2 + 1, :]
    tail[4:5, :] = ids[...].astype(F32)
    for c in range(ST // 128):
        cols = slice(128 * c, 128 * c + 128)
        block = jnp.concatenate(
            [weights[pl.ds(pl.multiple_of((x + q) % 4 * 16, 16), 16), cols] for q in range(DIRECT // 16)]
            + [tail[:, cols], jnp.zeros((120 - DIRECT, 128), F32)],
            axis=0,
        )
        rows[cols, :] = block.T

    copy.wait()

    def move(i, carry):
        for j in range(16):
            pair = spots[i // 16, i % 16 * 16 + j]
            placed[pl.ds(pair & 65535, 1), :] = rows[pl.ds(i * 16 + j, 1), :]
            placed[pl.ds(pair >> 16, 1), :] = rows[pl.ds(ST // 2 + i * 16 + j, 1), :]
        return carry

    lax.fori_loop(0, ST // 32, move, 0)


def place(owner, ids, weights, records):
    return pl.pallas_call(
        place_kernel,
        out_shape=jax.ShapeDtypeStruct((SLABS * CAP, 128), F32),
        in_specs=[HBM] * 4,
        out_specs=VM,
        scratch_shapes=[
            pltpu.VMEM((1, ST), jnp.int32),
            pltpu.VMEM((1, ST), jnp.int32),
            pltpu.VMEM((64, ST), F32),
            pltpu.VMEM((2, 2, ST), F32),
            pltpu.VMEM((8, ST), F32),
            pltpu.VMEM((ST, 128), F32),
            pltpu.VMEM((4, 256), jnp.int32),
            pltpu.SMEM((4, 256), jnp.int32),
            DMA,
            DMA((4,)),
        ],
        compiler_params=pltpu.CompilerParams(vmem_limit_bytes=12 << 20),
        name="place",
    )(owner, ids, weights, records)


def wave_shift(w):
    return w + w // 2 - 2 * (w // 3)


def turn_stations(w, placed, send_w, send_r):
    me, ev, y, z, c, x, half = coords()
    base = (y + wave_shift(w)) % 4 * 8

    def block(t, carry):
        slab = base + t
        for h in range(2):
            turned = placed[pl.ds(pl.multiple_of(slab * CAP + h * 128, 128), 128), :].T
            send_w[slab, :, 128 * h : 128 * h + 128] = turned[:DIRECT]
            for r in range(5):
                send_r[slab, :, 256 * r + 128 * h : 256 * r + 128 * h + 128] = turned[DIRECT + r : DIRECT + r + 1]
        return carry

    lax.fori_loop(0, 8, block, 0)


def weight_goal(dy, dz):
    me, ev, y, z, c, x, half = coords()
    deep = half * 4 + z
    step = (0, 1, 7)[dz] if dz < 3 else 2 + 4 * ((deep // 2 + dy) % 2)
    deep = (deep + step) % 8
    return (y + dy) % 4 * 8 + deep % 4 * 2, x * 2 + deep // 4


def record_goal(dy, dz):
    me, ev, y, z, c, x, half = coords()
    return (y + dy) % 4 * 8 + (z + (0, 1, 3, 2)[dz]) % 4 * 2


def greet_stations(barrier):
    me, ev, y, z, c, x, half = coords()
    for dy in range(4):
        for dz in range(4):
            if dy == 0 and dz == 0:
                signal(barrier, 2, space=me + 1 - 2 * c)
                continue
            goal, event = weight_goal(dy, dz)
            other = record_goal(dy, dz)
            for c2 in range(2):
                signal(barrier, space=goal + c2, event=event)
                signal(barrier, space=other + c2)
    signal(barrier, event=(ev + 2) % 8)
    signal(barrier, event=(ev + 6) % 8)
    return 64


def own_stations(send_w, send_r, got_w, got_r, rw, rr):
    me, ev, y, z, c, x, half = coords()
    here = (0, 0, c)
    pltpu.make_async_copy(send_w.at[me], got_w.at[here], rw.at[here]).start()
    pltpu.make_async_copy(send_r.at[me], got_r.at[here], rr.at[here]).start()


def station_copies(w, first, send_w, send_r, got_w, got_r, sw, rw, sr, rr):
    me, ev, y, z, c, x, half = coords()
    copies = []
    for dz in range(4):
        for c2 in range(2):
            if first and dz == 0:
                if c2 == 0:
                    continue
                goal = other = me + 1 - 2 * c
                event = ev
            else:
                goal, event = weight_goal(wave_shift(w), dz)
                goal, other = goal + c2, record_goal(wave_shift(w), dz) + c2
            mine, there = (w, dz, c2), (w, dz, c)
            copies += [
                copy_to(send_w.at[goal], got_w.at[there], sw.at[mine], rw.at[there], space=goal, event=event),
                copy_to(send_r.at[other], got_r.at[there], sr.at[mine], rr.at[there], space=other),
            ]
    return copies


def share_copies(w, got_w, left, right, fs, fr):
    ev = lax.axis_index("event")
    return (
        copy_to(got_w.at[w, :, :, 0:16], left.at[w], fs.at[w, 0], fr.at[w, 0], event=(ev + 2) % 8),
        copy_to(got_w.at[w, :, :, 16:32], right.at[w], fs.at[w, 1], fr.at[w, 1], event=(ev + 6) % 8),
    )


def receive_stations(w, got_w, got_r, left, right, rw, rr, fs, fr):
    for dz in range(4):
        for cs in range(2):
            at = (w, dz, cs)
            pltpu.make_async_copy(got_w.at[at], got_w.at[at], rw.at[at]).wait()
            pltpu.make_async_copy(got_r.at[at], got_r.at[at], rr.at[at]).wait()
    for copy in share_copies(w, got_w, left, right, fs, fr):
        copy.start()


def gather_sources(got_w, got_r, left, right, left_part, onehot, total, receive, start, shares):
    def add(w, carry):
        def products(nodes, row, samples, cols):
            for q in range(4):
                product = nodes * samples[:, 256 * q : 256 * q + 256]
                upper = product.astype(jnp.bfloat16)
                at = row + 32 * q
                left_part[at : at + 32, cols] = upper
                left_part[at + 128 : at + 160, cols] = (product - upper.astype(F32)).astype(jnp.bfloat16)

        def direct(k, carry):
            at = (w, k // 2, k % 2)
            cols = pl.ds(pl.multiple_of(k * CAP, CAP), CAP)
            samples = got_r[at]
            products(got_w[at], 0, samples, cols)
            spot = samples[:, 1024:1280].astype(jnp.int32)
            for i in range(8):
                row = lax.broadcasted_iota(jnp.int32, (128, CAP), 0) + 128 * i
                onehot[128 * i : 128 * i + 128, cols] = jnp.where(row == spot, 1.0, 0.0).astype(jnp.bfloat16)
            return carry

        lax.fori_loop(0, 8, direct, 0)

        def shared(k, carry):
            at = (w, k // 2, k % 2)
            cols = pl.ds(pl.multiple_of(k * CAP, CAP), CAP)
            nodes = jnp.concatenate([right[at], left[at]], axis=0)
            products(nodes, 256, got_r[at], cols)
            return carry

        def columns(first, count):
            def body(j, carry):
                at = pl.ds(pl.multiple_of(j * 256, 256), 256)
                part = slice(first, first + count)
                total[j, part] = total[j, part] + lax.dot_general(
                    left_part[part, :], onehot[at, :], (((1,), (1,)), ((), ())), preferred_element_type=F32
                )
                return carry

            lax.fori_loop(0, 4, body, 0)

        @pl.when(w < 3)
        def _():
            receive(w + 1)

        if EARLY == 2:
            pl.when(w == 0)(lambda: start(3))

        @pl.when(w == 3)
        def _():
            columns(0, 256)

        for copy in shares(w):
            copy.wait_recv()
        lax.fori_loop(0, 8, shared, 0)

        @pl.when(w < 3)
        def _():
            columns(0, 512)

        @pl.when(w == 3)
        def _():
            columns(256, 256)

        return carry

    total[...] = jnp.zeros_like(total)
    lax.fori_loop(0, 4, add, 0)


def spread_sources(total, src):
    x = lax.axis_index("event") // 2

    def tile(i, carry):
        q, r = i // 8, i % 8
        goal = q * 8 + (r // 2 + x) % 4 * 2 + r % 2
        row = r // 4 * 256 + q * 32 + r % 4 * 8
        upper, lower = pl.ds(pl.multiple_of(row, 8), 8), pl.ds(pl.multiple_of(row + 128, 8), 8)
        sums = [total[j, upper, :] + total[j, lower, :] for j in range(4)]
        for j in range(8):
            src[pl.ds(pl.multiple_of(goal * 64 + j * 8, 8), 8), :] = sums[j // 2][:, j % 2 * 128 : j % 2 * 128 + 128]
        return carry

    lax.fori_loop(0, 32, tile, 0)


def row_of(n):
    return n // 8 * 64 + n % 8


def strided(base):
    return pl.ds(base, 8, stride=8)


def tile_of(n):
    return pl.ds(pl.multiple_of(n * 8, 8), 8)


def each_node(body):
    def group(g, carry):
        for r in range(8):
            body(g * 8 + r, g * 64 + r)
        return carry

    lax.fori_loop(0, 8, group, 0)


def element_masks():
    sub = lax.broadcasted_iota(jnp.int32, (8, 128), 0)
    lane = lax.broadcasted_iota(jnp.int32, (8, 128), 1)
    return sub, lane


def from_before_x(v):
    sub, lane = element_masks()
    return jnp.where((lane & 15) != 0, pltpu.roll(v, 1, 1), 0.0)


def from_before_y(v):
    sub, lane = element_masks()
    turned = pltpu.roll(v, 16, 1)
    moved = jnp.where(lane < 16, pltpu.roll(turned, 1, 0), turned)
    return jnp.where(((sub & 1) != 0) | (lane >= 16), moved, 0.0)


def after_x(v, old):
    sub, lane = element_masks()
    return jnp.where((lane & 15) != 15, pltpu.roll(v, 127, 1), old)


def after_y(v, old):
    sub, lane = element_masks()
    turned = pltpu.roll(v, 112, 1)
    moved = jnp.where(lane >= 112, pltpu.roll(turned, 7, 0), turned)
    return jnp.where(((sub & 1) != 1) | (lane < 112), moved, old)


def stiffness(now, local, stiff, terms, first, fields=(0, 1, 2, 3)):
    def line(nodes, fresh, fresh_terms):
        mu = [stiff[n] for n in nodes]
        sums = [None] * 4
        for e in range(2):
            g = []
            for f in (e, e + 2):
                if f not in fields and 2 not in fields:
                    continue
                grad = gradient([now[f * 64 + n] for n in nodes])
                g.append(grad)
                if f not in fields:
                    continue
                out = divergence([a * b for a, b in zip(grad, mu)])
                for n, value in zip(nodes, out):
                    local[f * 64 + n] = value if fresh else local[f * 64 + n] + value
            if 2 in fields:
                for i in range(4):
                    pair = g[0][i] * g[1][i]
                    sums[i] = pair if e == 0 else sums[i] + pair
        if 2 in fields:
            for n, value in zip(nodes, sums):
                terms[tile_of(n), :] = value if fresh_terms else terms[tile_of(n), :] + value

    def along_a(l, carry):
        line([4 * l + i for i in range(4)], True, first)
        return carry

    def along_b(l, carry):
        line([l // 4 * 16 + l % 4 + 4 * i for i in range(4)], False, False)
        return carry

    def along_c(l, carry):
        line([l + 16 * i for i in range(4)], False, False)
        return carry

    for body in (along_a, along_b, along_c):
        lax.fori_loop(0, 16, body, 0)


def assemble_xy(local, first, count):
    def along(gap, node_of, from_before, after):
        def lines(i, carry):
            at = [first * 64 + i * 64 + node_of(k) for k in range(16)]
            low, high = [local[n] for n in at], [local[n + gap] for n in at]
            new = [a + from_before(b) for a, b in zip(low, high)]
            end = [after(a, b) for a, b in zip(new, high)]
            for n, a, b in zip(at, new, end):
                local[n] = a
                local[n + gap] = b
            return carry

        lax.fori_loop(0, count, lines, 0)

    along(3, lambda l: 4 * l, from_before_x, after_x)
    along(12, lambda l: l // 4 * 16 + l % 4, from_before_y, after_y)


def pack_faces(local, faces, first, count):
    sub, lane = element_masks()

    def group(i, carry):
        base = i // 4 * 64 + i % 4 * 4
        low = local[base]
        high = pltpu.roll(local[base + 48], 2, 0)
        for q in range(1, 4):
            low = jnp.where((sub >> 1) == q, pltpu.roll(local[base + q], 2 * q, 0), low)
            high = jnp.where((sub >> 1) == q, pltpu.roll(local[base + 48 + q], (2 * q + 2) % 8, 0), high)
        faces[0, i] = low
        faces[1, i] = high
        return carry

    lax.fori_loop(first * 4, first * 4 + count * 4, group, 0)


def assemble_z(local, got, first, count):
    me = lax.axis_index("space")
    sub, lane = element_masks()

    def group(i, carry):
        base = i // 4 * 64 + i % 4 * 4
        before = jnp.where(me > 0, got[0, i], 0.0)
        after = jnp.where(me < SLABS - 1, got[1, i], 0.0)
        for q in range(4):
            low, high = local[base + q], local[base + 48 + q]
            mine = pltpu.roll(before, (8 - 2 * q) % 8, 0) if q else before
            new = low + jnp.where(sub < 2, mine, pltpu.roll(high, 2, 0))
            theirs = pltpu.roll(after, (6 - 2 * q) % 8, 0) if q < 3 else after
            local[base + q] = new
            local[base + 48 + q] = jnp.where(sub < 6, pltpu.roll(new, 6, 0), high + theirs)
        return carry

    lax.fori_loop(first * 4, first * 4 + count * 4, group, 0)


def inverse_mass(density, got, inv):
    me = lax.axis_index("space")
    sub, lane = element_masks()

    def planes(v):
        out = []
        low = v + from_before_x(v)
        for a in (low, v, after_x(low, v)):
            new = a + from_before_y(a)
            out += [(new, a, after_y(new, a))]
        return out

    here = planes(density)
    before = planes(jnp.where(me > 0, got[0], 0.0))
    after = planes(jnp.where(me < SLABS - 1, got[1], 0.0))
    for a in range(3):
        for b in range(3):
            v = here[a][b]
            low = v + jnp.where(sub < 2, pltpu.roll(before[a][b], 2, 0), pltpu.roll(v, 2, 0))
            high = v + jnp.where(sub < 6, pltpu.roll(v, 6, 0), pltpu.roll(after[a][b], 6, 0))
            for c, value in enumerate((low, v, high)):
                inverse = 1.0 / value
                for n in range(64):
                    at = n % 4, n // 4 % 4, n // 16
                    if tuple((i + 1) // 2 for i in at) == (a, b, c):
                        weight = np.prod([1.2 if i in (1, 2) else 6.0 for i in at])
                        inv[n] = inverse * np.float32(STEP_SQUARE * weight)


def step_kernel(
    placed, fwd_now_h, fwd_prev_h, adj_now_h, adj_prev_h, shear_h, density,
    fwd_last, fwd_before, adj_last, adj_before, pieces,
    fwd_now, fwd_prev, adj_now, adj_prev, shear, send_w, send_r,
    got_w, got_r, left, right, left_part, onehot, total, src,
    zero, one, local, stiff, inv, terms, faces, got_faces, got_density, out_terms, got_terms,
    sw, rw, sr, rr, fs, fr, hs, hr, ds, dr, ts, tr, ins,
):
    pairs = (
        (fwd_now_h, fwd_now), (adj_now_h, adj_now), (shear_h, shear), (fwd_prev_h, fwd_prev), (adj_prev_h, adj_prev)
    )
    fetch = [pltpu.make_async_copy(a, b, ins.at[k]) for k, (a, b) in enumerate(pairs)]
    for copy in fetch:
        copy.start()
    me, ev, y, z, c, x, half = coords()
    up, down = (me + 1) % SLABS, (me + SLABS - 1) % SLABS
    barrier = pltpu.get_barrier_semaphore()
    greeted = greet_stations(barrier)
    for k in range(1, 4):
        signal(barrier, event=(ev + 2 * k) % EVENT)
    signal(barrier, event=x * 2 + 1 - half)
    signal(barrier, space=up)
    signal(barrier, space=down)

    def turn(w):
        turn_stations(w, placed, send_w, send_r)

    turn(0)
    pl.semaphore_wait(barrier, greeted + 4 + 2)

    weigh = [
        copy_to(density, got_density.at[1], ds.at[1], dr.at[1], space=down),
        copy_to(density, got_density.at[0], ds.at[0], dr.at[0], space=up),
    ]
    for copy in weigh:
        copy.start()
    stations = (send_w, send_r, got_w, got_r, sw, rw, sr, rr)

    def start(w):
        for copy in station_copies(w, False, *stations):
            copy.start()

    def receive(w):
        receive_stations(w, got_w, got_r, left, right, rw, rr, fs, fr)

    def shares(w):
        return share_copies(w, got_w, left, right, fs, fr)

    first_wave = station_copies(0, True, *stations)
    for copy in first_wave:
        copy.start()
    own_stations(send_w, send_r, got_w, got_r, rw, rr)
    for w in range(1, EARLY):
        turn(w)
        start(w)

    for copy in fetch:
        copy.wait()

    def load(g, carry):
        for r in range(8):
            n, row = g * 8 + r, g * 64 + r
            for f, ref in enumerate((fwd_now, adj_now)):
                for e in range(2):
                    zero[(2 * f + e) * 64 + n] = ref[strided(e * 512 + row), :]
            along_a = np.float32((1.0 / 6.0, 5.0 / 6.0, 5.0 / 6.0, 1.0 / 6.0)[r % 4])
            stiff[n] = shear[strided(row), :] * (point_weight((2 * g + r // 4) % 4) * point_weight(g // 2) * along_a)
        return carry

    lax.fori_loop(0, 8, load, 0)

    def exchange(step, first, count):
        assemble_xy(local, first, count)
        pack_faces(local, faces.at[step], first, count)
        at, k = slice(first * 4, first * 4 + count * 4), first // 2
        halo = [
            copy_to(faces.at[step, 0, at], got_faces.at[step, 1, at], hs.at[step, k, 0], hr.at[step, k, 0], space=down),
            copy_to(faces.at[step, 1, at], got_faces.at[step, 0, at], hs.at[step, k, 1], hr.at[step, k, 1], space=up),
        ]
        for copy in halo:
            copy.start()
        return halo

    def advance(step, first, count):
        assemble_z(local, got_faces.at[step], first, count)

        def update(n, row):
            mine = inv[n]
            for f in range(first, first + count):
                at, rows = f * 64 + n, strided(f % 2 * 512 + row)
                if step == 0:
                    old = (fwd_prev, adj_prev)[f // 2][rows, :]
                    new = 2.0 * zero[at] - old - local[at] * mine
                    one[at] = new
                    (fwd_before, adj_before)[f // 2][rows, :] = new
                else:
                    (fwd_last, adj_last)[f // 2][rows, :] = 2.0 * one[at] - zero[at] - local[at] * mine

        each_node(update)

    def subtract(step):
        def less(n, row):
            for e in range(2):
                at = (2 + e) * 64 + n
                local[at] = local[at] - src[strided((2 * e + step) * 512 + row), :]

        each_node(less)

    def arrived(copies):
        for copy in copies:
            copy.wait_recv()

    stiffness(zero, local, stiff, terms, True)
    forward = exchange(0, 0, 2)
    arrived(weigh)
    inverse_mass(density[...], got_density, inv)
    for w in range(EARLY, 4):
        turn(w)
    receive(0)
    if EARLY < 4:
        start(EARLY)
    gather_sources(got_w, got_r, left, right, left_part, onehot, total, receive, start, shares)
    spread_sources(total, src)
    subtract(0)
    adjoint = exchange(0, 2, 2)

    arrived(forward)
    advance(0, 0, 2)
    stiffness(one, local, stiff, terms, False, (0, 1))
    forward_last = exchange(1, 0, 2)

    arrived(adjoint)
    advance(0, 2, 2)
    stiffness(one, local, stiff, terms, False, (2, 3))

    def cut(j, carry):
        out_terms[j] = terms[pl.ds(j, 64, stride=8), :]
        return carry

    lax.fori_loop(0, EVENT, cut, 0)
    given = []
    for k in range(1, 4):
        goal = (x + k) % 4 * 2
        given.append(
            copy_to(out_terms.at[pl.ds(goal, 2)], got_terms.at[k], ts.at[k], tr.at[k], event=goal + half)
        )
        given[-1].start()
    subtract(1)
    adjoint_last = exchange(1, 2, 2)
    arrived(forward_last)
    advance(1, 0, 2)

    arrived(given)
    for h in range(2):
        got_terms[0, h] = out_terms[x * 2 + h] + got_terms[1, h] + got_terms[2, h] + got_terms[3, h]
    other = copy_to(got_terms.at[0, 1 - half], pieces.at[1], ts.at[0], tr.at[0], event=x * 2 + 1 - half)
    other.start()
    pieces[0] = got_terms[0, half]
    arrived(adjoint_last)
    advance(1, 2, 2)
    other.wait_recv()
    given.append(other)

    for copy in first_wave + weigh + forward + adjoint + forward_last + adjoint_last + given:
        copy.wait_send()

    def last(w, carry):
        for copy in station_copies(w, False, *stations):
            copy.wait_send()
        return carry

    lax.fori_loop(1, 4, last, 0)

    def last_shares(w, carry):
        for copy in shares(w):
            copy.wait_send()
        return carry

    lax.fori_loop(0, 4, last_shares, 0)


def steps(placed, fwd_now, fwd_prev, adj_now, adj_prev, shear, density):
    fields = pltpu.VMEM((256, 8, 128), F32)
    waves = DMA((4, 4, 2))
    return pl.pallas_call(
        step_kernel,
        out_shape=(
            *[jax.ShapeDtypeStruct((1024, 128), F32)] * 4,
            jax.ShapeDtypeStruct((2, 64, 128), F32),
        ),
        in_specs=[VM, HBM, HBM, HBM, HBM, HBM, VM],
        out_specs=(VM,) * 5,
        scratch_shapes=[
            *[pltpu.VMEM((1024, 128), F32)] * 4,
            pltpu.VMEM((512, 128), F32),
            pltpu.VMEM((SLABS, DIRECT, CAP), F32),
            pltpu.VMEM((SLABS, 1, 5 * CAP), F32),
            pltpu.VMEM((4, 4, 2, DIRECT, CAP), F32),
            pltpu.VMEM((4, 4, 2, 1, 5 * CAP), F32),
            pltpu.VMEM((4, 4, 2, 16, CAP), F32),
            pltpu.VMEM((4, 4, 2, 16, CAP), F32),
            pltpu.VMEM((512, 8 * CAP), jnp.bfloat16),
            pltpu.VMEM((ELEMS, 8 * CAP), jnp.bfloat16),
            pltpu.VMEM((4, 512, 256), F32),
            pltpu.VMEM((2048, 128), F32),
            fields,
            fields,
            fields,
            pltpu.VMEM((64, 8, 128), F32),
            pltpu.VMEM((64, 8, 128), F32),
            pltpu.VMEM((512, 128), F32),
            pltpu.VMEM((2, 2, 16, 8, 128), F32),
            pltpu.VMEM((2, 2, 16, 8, 128), F32),
            pltpu.VMEM((2, 8, 128), F32),
            pltpu.VMEM((EVENT, 64, 128), F32),
            pltpu.VMEM((4, 2, 64, 128), F32),
            waves, waves, waves, waves,
            DMA((4, 2)), DMA((4, 2)),
            DMA((2, 2, 2)), DMA((2, 2, 2)),
            DMA((2,)), DMA((2,)),
            DMA((4,)), DMA((4,)),
            DMA((5,)),
        ],
        compiler_params=pltpu.CompilerParams(collective_id=0, has_side_effects=True, vmem_limit_bytes=32 << 20),
        name="steps",
    )(placed, fwd_now, fwd_prev, adj_now, adj_prev, shear, density)


def finish_kernel(a, b, c, d, pieces, shear, a_out, b_out, c_out, d_out, kernel_out, kernel, sems):
    ev = lax.axis_index("event")
    copies = [
        pltpu.make_async_copy(src, dst, sems.at[k])
        for k, (src, dst) in enumerate(((a, a_out), (b, b_out), (c, c_out), (d, d_out), (kernel, kernel_out)))
    ]
    for copy in copies[:4]:
        copy.start()
    for i in range(8):
        rows = slice(8 * i, 8 * i + 8)
        total = pieces[0, rows] + pieces[1, rows]
        n = 8 * i + lax.broadcasted_iota(jnp.int32, (8, 128), 0)
        edge = [((n >> 2 * k) & 3) * (3 - ((n >> 2 * k) & 3)) == 0 for k in range(3)]
        weight = [jnp.where(e, np.float32(1.0 / 6.0), np.float32(5.0 / 6.0)) for e in edge]
        factor = weight[0] * weight[1] * weight[2] * np.float32(-TIME_STEP)
        kernel[rows, :] = total * (factor * shear[pl.ds(pl.multiple_of(i * 64 + ev * 8, 8), 8), :])
    copies[4].start()
    for copy in copies:
        copy.wait()


def finish(*given):
    return pl.pallas_call(
        finish_kernel,
        out_shape=(*[jax.ShapeDtypeStruct((1024, 128), F32)] * 4, jax.ShapeDtypeStruct((64, 128), F32)),
        in_specs=[VM] * 6,
        out_specs=(HBM,) * 5,
        scratch_shapes=[pltpu.VMEM((64, 128), F32), DMA((5,))],
        compiler_params=pltpu.CompilerParams(vmem_limit_bytes=8 << 20),
        name="finish",
    )(*given)


def to_rows(field):
    count = field.size // (64 * ELEMS)
    return field.reshape(count, 8, 8, 8, 128).transpose(0, 1, 3, 2, 4).reshape(count * 512, 128)


def from_rows(rows):
    return rows.reshape(2, 8, 8, 8, 128).transpose(0, 1, 3, 2, 4).reshape(2, 64, ELEMS)


def shards(
    fwd_now, fwd_prev, adj_now, adj_prev, shear_mod, density, station_owner, receiver_local, station_weights, adj_records
):
    def far(value):
        return pltpu.with_memory_space_constraint(value, pltpu.HBM)

    shear = to_rows(shear_mod)
    placed = place(
        far(station_owner.T), far(receiver_local.reshape(1, ST)), far(station_weights), far(adj_records)
    )
    found = steps(
        placed, *[far(to_rows(v)) for v in (fwd_now, fwd_prev, adj_now, adj_prev)],
        shear, density.reshape(8, 128),
    )
    *fields, kernel = finish(*found, shear)
    return (*map(from_rows, fields), kernel)


def solution(mesh):
    fields = P("event", None, "space")
    return jax.shard_map(
        shards,
        mesh=mesh,
        in_specs=(
            fields, fields, fields, fields,
            P(None, "space"), P("space"), P("space", None), P("space"), P(None, "space"), fields,
        ),
        out_specs=(fields, fields, fields, fields, P(None, ("space", "event"))),
        check_vma=False,
    )
```
